32 devices in a mesh: req: 8 (over z, x), cfg: 2 (over core), seq: 2 (over y).
Axes of the slice: x: 2, y: 2, z: 4, core: 2. Of those that a mesh axis runs over, the one named last changes fastest.
Arguments:
- queries: bfloat16 [8, 2, 512, 1024], P('req', 'cfg', 'seq'), may hold values from -48 to 48
- key_vectors: bfloat16 [8, 2, 512, 1024], P('req', 'cfg', 'seq'), may hold values from -48 to 48
- values: bfloat16 [8, 2, 512, 1024], P('req', 'cfg', 'seq'), may hold values from -6 to 6
- hidden: bfloat16 [8, 2, 512, 1536], P('req', 'cfg', 'seq'), may hold values from -15 to 15
- out_proj: bfloat16 [1024, 1536], P('req'), may hold values from -0.1875 to 0.1875
- head_weight: bfloat16 [1536, 64], replicated, may hold values from -0.15625 to 0.15625
- head_bias: float32 [64], replicated, may hold values from -3 to 3
- attn_gate: float32 [8, 1536], P('req'), may hold values from 0.5 to 4
- shift_scale: float32 [8, 2, 1536], P('req'), may hold values from -3 to 3
- grid_shape: int32 [8, 3], P('req'), may hold values from 1 to 32, as said below
- step_index: int32 [8], P('req'), may hold values from 0 to 19
- guide_scale: float32 [8], P('req'), may hold values from 3 to 6
- latent: float32 [8, 512, 64], P('req', 'seq', 'cfg'), may hold values from -6 to 6
Outputs:
- next_latent: float32 [8, 512, 64], P('req', 'seq', 'cfg')
- velocity: float32 [8, 512, 64], P('req', 'seq', 'cfg')
The draws below stay inside these ranges and needn't reach their ends.
Inputs may be any that keep to these rules, and one draw needn't show every extreme that they name: `grid_shape`: the frames are at most 2, the height at most 8 and the width at most 32, so that frames * height * width is at most 512; in every draw some request fills all 512 slots.
All inputs are finite; a program needn't handle non-finite values.
Results may differ from the reference program's by a relative error of at most 0.0052.
Values may be sent and summed in bfloat16 or wider, within the bound.
A program may use at most 64 MiB of HBM per device.

```python
import math
import jax
import jax.numpy as jnp
from jax import lax

D = 1536
HEADS = 8
HEAD_DIM = 128
CH = 64
STEPS = 20
TOK_DEV = 256
SEQ_LEN = 512
REQS = 8


def draw_queries(key, part):
    shape = (REQS, 2, SEQ_LEN, HEADS * HEAD_DIM)
    subkey = jax.random.fold_in(key, 11)
    base = jnp.clip(2.0 * jax.random.normal(subkey, shape, jnp.float32), -12.0, 12.0)
    return base.astype(jnp.bfloat16)


def draw_key_vectors(key, part):
    shape = (REQS, 2, SEQ_LEN, HEADS * HEAD_DIM)
    subkey = jax.random.fold_in(key, 23)
    base = jnp.clip(jax.random.normal(subkey, shape, jnp.float32), -6.0, 6.0)
    return base.astype(jnp.bfloat16)


def draw_hidden(key, part):
    subkeys = jax.random.split(jax.random.fold_in(key, 37), 3)
    low = math.log(0.5)
    high = math.log(5.0)
    row_scale = jnp.exp(jax.random.uniform(subkeys[0], (REQS, 2, SEQ_LEN, 1), jnp.float32, low, high))
    col_scale = jnp.exp(jax.random.uniform(subkeys[1], (1, 1, 1, D), jnp.float32, low, high))
    shape = (REQS, 2, SEQ_LEN, D)
    base = jnp.clip(jax.random.normal(subkeys[2], shape, jnp.float32), -4.0, 4.0)
    return (0.15 * row_scale * col_scale * base).astype(jnp.bfloat16)


def draw_grid_shape(key, part):
    subkeys = jax.random.split(jax.random.fold_in(key, 41), 4)
    most_frames = SEQ_LEN // TOK_DEV
    frames = jax.random.randint(subkeys[0], (REQS,), max(1, most_frames // 2), most_frames + 1)
    height = jax.random.randint(subkeys[1], (REQS,), 4, 9)
    across = jax.random.randint(subkeys[2], (REQS,), max(1, TOK_DEV // 16), TOK_DEV // 8 + 1)
    chosen = jax.random.randint(subkeys[3], (), 0, REQS)
    filled = jnp.arange(REQS, dtype=jnp.int32) == chosen
    frames = jnp.where(filled, most_frames, frames)
    height = jnp.where(filled, 8, height)
    across = jnp.where(filled, TOK_DEV // 8, across)
    return jnp.stack([frames, height, across], axis=1).astype(jnp.int32)


def touch_ends(drawn, own_key, smallest, top_value):
    place = [jax.random.randint(jax.random.fold_in(own_key, axis), (), 0, length) for axis, length in enumerate(drawn.shape)]
    widest = drawn.shape.index(max(drawn.shape))
    next_to = place[:widest] + [(place[widest] + 1) % drawn.shape[widest]] + place[widest + 1:]
    return drawn.at[tuple(place)].set(smallest).at[tuple(next_to)].set(top_value)


def block_scale(key, shape, cuts, least, largest):
    gain, own = 1.0, jax.random.fold_in(key, 6)
    for dim, shards_of in cuts:
        draws = jnp.exp(jax.random.uniform(jax.random.fold_in(own, dim), (shards_of,), jnp.float32, least / len(cuts), largest / len(cuts)))
        gain = gain * jnp.repeat(draws, shape[dim] // shards_of).reshape([-1 if axis == dim else 1 for axis in range(len(shape))])
    return gain


def normal_values(own_key, dims, scale, reach, shards=(), kind=jnp.bfloat16):
    drawn = scale * jax.random.normal(own_key, dims, jnp.float32)
    if shards:
        drawn = drawn * block_scale(own_key, dims, shards, -0.22, 0.18)
    return jnp.clip(drawn, -reach, reach).astype(kind)


def setup_inputs(seed: int = 0) -> dict:
    key_list = jax.random.split(jax.random.key(seed), 14)
    return {
        "queries": draw_queries(jax.random.fold_in(key_list[13], 71), 0),
        "key_vectors": draw_key_vectors(jax.random.fold_in(key_list[13], 71), 0),
        "values": normal_values(key_list[2], (REQS, 2, SEQ_LEN, HEADS * HEAD_DIM), 1.0, 6.0, ((0, 8), (1, 2), (2, 2))),
        "hidden": draw_hidden(jax.random.fold_in(key_list[13], 71), 0),
        "out_proj": normal_values(key_list[4], (HEADS * HEAD_DIM, D), (HEADS * HEAD_DIM) ** -0.5, 0.1875, ((0, 8),)),
        "head_weight": normal_values(key_list[5], (D, CH), D ** -0.5, 0.15625),
        "head_bias": normal_values(key_list[6], (CH,), 0.5, 3.0, (), jnp.float32),
        "attn_gate": jnp.clip(jnp.exp(math.log(4.0) - 2.0794415 * jax.random.uniform(key_list[7], (REQS, D), jnp.float32) ** block_scale(key_list[7], (REQS, D), ((0, 8),), -0.2, 0.2)), 0.5, 4.0),
        "shift_scale": normal_values(key_list[8], (REQS, 2, D), 0.5, 3.0, ((0, 8),), jnp.float32),
        "grid_shape": draw_grid_shape(jax.random.fold_in(key_list[13], 71), 0),
        "step_index": touch_ends(jax.random.randint(key_list[10], (REQS,), 0, STEPS), jax.random.fold_in(key_list[10], 1), 0, STEPS - 1).astype(jnp.int32),
        "guide_scale": jnp.clip(3.0 + 3.0 * jax.random.uniform(key_list[11], (REQS,), jnp.float32) ** block_scale(key_list[11], (REQS,), ((0, 8),), -0.2, 0.2), 3.0, 6.0),
        "latent": normal_values(key_list[12], (REQS, SEQ_LEN, CH), 1.0, 6.0, ((0, 8), (1, 2), (2, 2)), jnp.float32),
    }


masked_score = -1e+30
norm_eps = 1e-06
shift_factor = 5.0

def rotary(vectors, grid_dims, first_token):
    row_count, col_count = vectors.shape
    sixth_dim = HEAD_DIM // 6
    time_pairs = (HEAD_DIM - 4 * sixth_dim) // 2
    column = jnp.arange(col_count, dtype=jnp.int32) % HEAD_DIM
    pair_index = column // 2
    space_pair = (pair_index - time_pairs).astype(jnp.float32)
    is_time = pair_index < time_pairs
    is_height = jnp.logical_and(pair_index >= time_pairs, pair_index < time_pairs + sixth_dim)
    exponent = jnp.where(is_time, pair_index.astype(jnp.float32) / time_pairs, jnp.where(is_height, space_pair / sixth_dim, (space_pair - sixth_dim) / sixth_dim))
    frequency = jnp.power(jnp.float32(10000.0), -exponent)
    token_ids = first_token + jnp.arange(row_count, dtype=jnp.int32)
    plane_size = grid_dims[1] * grid_dims[2]
    frame_ids = token_ids // plane_size
    height = token_ids // grid_dims[2] % grid_dims[1]
    across = token_ids % grid_dims[2]
    position = jnp.where(is_time[None, :], frame_ids[:, None], jnp.where(is_height[None, :], height[:, None], across[:, None])).astype(jnp.float32)
    angles = position * frequency[None, :]
    is_even = column % 2 == 0
    source = vectors.astype(jnp.float32)
    partner = jnp.where(is_even[None, :], jnp.roll(source, -1, axis=1), jnp.roll(source, 1, axis=1))
    sign_flip = jnp.where(is_even, -1.0, 1.0).astype(jnp.float32)
    turned = source * jnp.cos(angles) + partner * (jnp.sin(angles) * sign_flip[None, :])
    return turned.astype(jnp.bfloat16)

def noise_level(step_value):
    progress = 1.0 - step_value.astype(jnp.float32) / STEPS
    return shift_factor * progress / (1.0 + (shift_factor - 1.0) * progress)

def output_head(hidden_rows, proj, gate_row, modulation, head_weight, head_bias):
    mixed_rows = hidden_rows.astype(jnp.float32) + gate_row[None, :] * proj
    average = lax.optimization_barrier(jnp.mean(mixed_rows, axis=-1, keepdims=True))
    centered = mixed_rows - average
    spread = lax.optimization_barrier(jnp.mean(centered * centered, axis=-1, keepdims=True))
    normed = centered * lax.rsqrt(spread + norm_eps)
    modded = (normed * (1.0 + modulation[1][None, :]) + modulation[0][None, :]).astype(jnp.bfloat16)
    return jnp.dot(modded, head_weight, preferred_element_type=jnp.float32) + head_bias[None, :]

def attend(rot_q, rot_k, value_rows, length):
    total_rows = rot_q.shape[0]
    block_rows = min(512, total_rows)
    score_scale = 1.0 / math.sqrt(HEAD_DIM)
    query_heads = rot_q.astype(jnp.float32).reshape(total_rows, HEADS, HEAD_DIM)
    key_heads = rot_k.astype(jnp.float32).reshape(total_rows, HEADS, HEAD_DIM)
    value_heads = value_rows.astype(jnp.float32).reshape(total_rows, HEADS, HEAD_DIM)
    live_keys = jnp.arange(total_rows, dtype=jnp.int32) < length

    def one_block(start):
        query_block = lax.dynamic_slice_in_dim(query_heads, start, block_rows, 0)
        scores = jnp.einsum('qhd,khd->hqk', query_block, key_heads) * score_scale
        scores = jnp.where(live_keys[None, None, :], scores, masked_score)
        row_max = lax.optimization_barrier(jnp.max(scores, axis=-1, keepdims=True))
        exponent = jnp.exp(scores - row_max)
        row_sum = lax.optimization_barrier(jnp.sum(exponent, axis=-1, keepdims=True))
        weights = lax.optimization_barrier((exponent / row_sum).astype(jnp.bfloat16))
        output = jnp.einsum('hqk,khd->qhd', weights.astype(jnp.float32), value_heads)
        return output.astype(jnp.bfloat16)
    starts = jnp.arange(total_rows // block_rows, dtype=jnp.int32) * block_rows
    blocks = lax.map(one_block, starts)
    return blocks.reshape(total_rows, HEADS * HEAD_DIM)

def reference(queries, key_vectors, values, hidden, out_proj, head_weight, head_bias, attn_gate, shift_scale, grid_shape, step_index, guide_scale, latent):

    def one_request(request_items):
        query_req, key_req, value_req, hidden_req, gate_row, modulation, grid_dims, step_value, guide_value, latent_req = request_items
        length = grid_dims[0] * grid_dims[1] * grid_dims[2]
        predictions = []
        for cfg_half in range(2):
            rot_q = lax.optimization_barrier(rotary(query_req[cfg_half], grid_dims, 0))
            rot_k = lax.optimization_barrier(rotary(key_req[cfg_half], grid_dims, 0))
            attended = attend(rot_q, rot_k, value_req[cfg_half], length)
            proj = jnp.dot(attended, out_proj, preferred_element_type=jnp.float32)
            predictions.append(output_head(hidden_req[cfg_half], proj, gate_row, modulation, head_weight, head_bias))
        guided = predictions[1] + guide_value * (predictions[0] - predictions[1])
        live_rows = jnp.arange(guided.shape[0], dtype=jnp.int32) < length
        velocity = jnp.where(live_rows[:, None], guided, jnp.float32(0.0))
        delta_level = noise_level(step_value + 1) - noise_level(step_value)
        return (latent_req + delta_level * velocity, velocity)
    return lax.map(one_request, (queries, key_vectors, values, hidden, attn_gate, shift_scale, grid_shape, step_index, guide_scale, latent))
```

```python
import functools
import math

import jax
import jax.numpy as jnp
from jax import lax
from jax.experimental import pallas as pl
from jax.experimental.pallas import tpu as pltpu
from jax.sharding import PartitionSpec as P

HEAD_DIM = 128
STEPS = 20
LANES = 128

masked_score = -1e30
norm_eps = 1e-06
shift_factor = 5.0
MESH = pl.DeviceIdType.MESH


def noise_level(step_value):
    progress = 1.0 - step_value / STEPS
    return shift_factor * progress / (1.0 + (shift_factor - 1.0) * progress)


def fill_tables(cos_ref, sin_ref, start, rows, first_token, dims):
    height, width = dims
    sixth = HEAD_DIM // 6
    time_pairs = (HEAD_DIM - 4 * sixth) // 2
    lane = lax.broadcasted_iota(jnp.int32, (8, HEAD_DIM), 1)
    pair = lane // 2
    is_time = pair < time_pairs
    is_row = pair < time_pairs + sixth
    pair_f = pair.astype(jnp.float32)
    space = pair_f - time_pairs
    exponent = jnp.where(
        is_time, pair_f / time_pairs, jnp.where(is_row, space / sixth, (space - sixth) / sixth)
    )
    freq = jnp.exp(exponent * -math.log(10000.0))[0:1]
    sign = jnp.where(lane % 2 == 0, -1.0, 1.0).astype(jnp.float32)[0:1]
    lanes = lax.broadcasted_iota(jnp.int32, (rows, HEAD_DIM), 1) // 2
    token = (first_token + lax.broadcasted_iota(jnp.int32, (rows, HEAD_DIM), 0)).astype(jnp.float32)
    h_vec = jnp.full((rows, HEAD_DIM), height.astype(jnp.float32))
    w_vec = jnp.full((rows, HEAD_DIM), width.astype(jnp.float32))
    frame = jnp.floor((token + 0.5) / (h_vec * w_vec))
    line = jnp.floor((token + 0.5) / w_vec)
    row = line - h_vec * jnp.floor((line + 0.5) / h_vec)
    col = token - w_vec * line
    position = jnp.where(lanes < time_pairs, frame, jnp.where(lanes < time_pairs + sixth, row, col))
    angles = position * freq
    cos_ref[start : start + rows, :] = jnp.cos(angles)
    sin_ref[start : start + rows, :] = jnp.sin(angles) * sign


def rotate(x, cos, sin, is_even):
    source = x.astype(jnp.float32)
    partner = jnp.where(
        is_even, pltpu.roll(source, HEAD_DIM - 1, 1), pltpu.roll(source, 1, 1)
    )
    return (source * cos + partner * sin).astype(jnp.bfloat16)


def kernel(
    n_seq,
    n_req,
    tail_rows,
    q_hbm,
    k_hbm,
    v_hbm,
    hidden_hbm,
    w_hbm,
    head_w_hbm,
    bias_hbm,
    gate_hbm,
    mod_hbm,
    grid_hbm,
    base_ref,
    gain_ref,
    qkv_buf,
    rot_buf,
    o_buf,
    att_buf,
    hid_buf,
    w_buf,
    cos_buf,
    sin_buf,
    pred_buf,
    other_buf,
    proj_buf,
    head_w,
    bias_ref,
    bias_col,
    gate_ref,
    mod_ref,
    grid_ref,
    load_sem,
    ready_sem,
    in_send,
    in_recv,
    o_send,
    o_recv,
    w_send,
    line_recv,
    x_recv,
    c_recv,
    p_send,
    p_recv,
):
    rows = hid_buf.shape[0]
    group = qkv_buf.shape[2]
    heads = group // HEAD_DIM
    total = n_seq * rows
    shard = w_hbm.shape[0]
    half = shard // 2
    subs = line_recv.shape[1]
    sub = half // subs
    line_len = n_req // 2
    me_s = lax.axis_index("seq")
    me_c = lax.axis_index("cfg")
    me_r = lax.axis_index("req")
    place = me_r // 2
    side_x = me_r % 2
    x_mate = me_r + 1 - 2 * side_x
    other = 1 - me_c
    below, above = jnp.maximum(me_r - 2, 0), jnp.minimum(me_r + 2, n_req - 1)
    has_below, has_above = place >= 1, place <= line_len - 2

    def remote(src, dst, s_sem, r_sem, **target):
        return pltpu.make_async_remote_copy(
            src_ref=src, dst_ref=dst, send_sem=s_sem, recv_sem=r_sem,
            device_id=target, device_id_type=MESH,
        )

    def drain(ref, sem):
        pltpu.make_async_copy(ref, ref, sem).wait()

    def signal(sem, **target):
        pl.semaphore_signal(sem, inc=1, device_id=target, device_id_type=MESH)

    barrier = pltpu.get_barrier_semaphore()
    for d in range(1, n_seq):
        signal(barrier, seq=lax.rem(me_s + d, n_seq))

    @pl.when(me_c == 0)
    def _():
        signal(barrier, cfg=other)

    @pl.when(has_above)
    def _():
        signal(barrier, req=above)

    @pl.when(side_x == 0)
    def _():
        signal(barrier, req=x_mate)

    def head_cols(owner, j):
        return pl.ds(pl.multiple_of(owner * group + j * HEAD_DIM, HEAD_DIM), HEAD_DIM)

    own_group = pl.ds(pl.multiple_of(me_s * group, group), group)
    loads = {
        "grid": pltpu.make_async_copy(grid_hbm, grid_ref, load_sem.at[0]),
        "k": pltpu.make_async_copy(k_hbm.at[:, own_group], qkv_buf.at[0, 0:rows, :], load_sem.at[1]),
        "q": pltpu.make_async_copy(q_hbm.at[:, own_group], qkv_buf.at[1, 0:rows, :], load_sem.at[1]),
        "v": pltpu.make_async_copy(v_hbm.at[:, own_group], qkv_buf.at[2, 0:rows, :], load_sem.at[1]),
        "w": pltpu.make_async_copy(
            w_hbm, w_buf.at[pl.ds(pl.multiple_of(me_r * shard, shard), shard), :], load_sem.at[2]
        ),
        "hidden": pltpu.make_async_copy(hidden_hbm, hid_buf, load_sem.at[3]),
        "head_w": pltpu.make_async_copy(head_w_hbm, head_w, load_sem.at[4]),
        "bias": pltpu.make_async_copy(bias_hbm, bias_ref, load_sem.at[5]),
        "gate": pltpu.make_async_copy(gate_hbm, gate_ref, load_sem.at[6]),
        "mod": pltpu.make_async_copy(mod_hbm, mod_ref, load_sem.at[7]),
    }
    loads["grid"].start()

    pl.semaphore_wait(
        barrier,
        n_seq - 1 + me_c + side_x + jnp.where(has_below, 1, 0),
    )

    def in_copy(d, j, kind):
        owner = lax.rem(me_s + d, n_seq)
        src = (k_hbm, q_hbm, v_hbm)[kind].at[:, head_cols(owner, j)]
        dst = qkv_buf.at[kind, d * rows : (d + 1) * rows, j * HEAD_DIM : (j + 1) * HEAD_DIM]
        return remote(src, dst, in_send, in_recv.at[d - 1, j], seq=owner)

    for j in range(heads):
        for d in range(1, n_seq):
            for kind in range(3):
                in_copy(d, j, kind).start()

    @pl.when(me_c == 1)
    def _():
        signal(ready_sem.at[0], cfg=other)

    @pl.when(has_below)
    def _():
        signal(ready_sem.at[1], req=below)

    @pl.when(side_x == 1)
    def _():
        signal(ready_sem.at[2], req=x_mate)

    for name, load in loads.items():
        if name != "grid":
            load.start()

    def piece(owner, which, u):
        start = pl.multiple_of(owner * shard + which * half + u * sub, sub)
        return w_buf.at[pl.ds(start, sub), :]

    def own_src(u):
        return w_hbm.at[pl.ds(pl.multiple_of(me_c * half + u * sub, sub), sub), :]

    def toward(side):
        return below if side == 0 else above

    def can_pass(side):
        return has_below if side == 0 else has_above

    def comes(side, k):
        return place + k <= line_len - 1 if side == 0 else place - k >= 0

    def owner_of(base, side, k):
        return base + 2 * k if side == 0 else base - 2 * k

    def line_copy(src, owner, side, u):
        return remote(src, piece(owner, me_c, u), w_send, line_recv.at[owner // 2, u], req=toward(side))

    def x_copy(src, owner, u):
        return remote(src, piece(owner, me_c, u), w_send, x_recv.at[owner // 2, u], req=x_mate)

    def c_copy(owner, u):
        return remote(piece(owner, me_c, u), piece(owner, me_c, u), w_send, c_recv, cfg=other)

    @pl.when(has_above)
    def _():
        pl.semaphore_wait(ready_sem.at[1], 1)

    for u in range(subs):
        for side in range(2):
            @pl.when(can_pass(side))
            def _():
                line_copy(own_src(u), me_r, side, u).start()

    @pl.when(side_x == 0)
    def _():
        pl.semaphore_wait(ready_sem.at[2], 1)

    for u in range(subs):
        x_copy(own_src(u), me_r, u).start()

    @pl.when(me_c == 0)
    def _():
        pl.semaphore_wait(ready_sem.at[0], 1)

    def line_step(k, u):
        for side in range(2):
            @pl.when(comes(side, k))
            def _():
                owner = owner_of(me_r, side, k)
                line_copy(piece(owner, me_c, u), owner, side, u).wait_recv()
                if k < line_len - 1:
                    @pl.when(can_pass(side))
                    def _():
                        line_copy(piece(owner, me_c, u), owner, side, u).start()
                x_copy(piece(owner, me_c, u), owner, u).start()
                c_copy(owner, u).start()

    def x_step(k, u):
        for side in range(2 if k else 1):
            @pl.when(comes(side, k))
            def _():
                owner = owner_of(x_mate, side, k)
                x_copy(piece(owner, me_c, u), owner, u).wait_recv()
                c_copy(owner, u).start()

    def finish_gather():
        drain(w_buf.at[0 : (n_req - 1) * half, :], c_recv)

    slots = heads * n_seq
    relays = {slot: [] for slot in range(-1, slots)}
    line_steps = [(k, u) for k in range(1, line_len) for u in range(subs)]
    x_steps = [(k, u) for k in range(line_len) for u in range(subs)]
    for i, (k, u) in enumerate(line_steps):
        relays[i * (5 * slots // 8) // len(line_steps) - 1].append((line_step, k, u))
    for i, (k, u) in enumerate(x_steps):
        relays[i * slots // len(x_steps)].append((x_step, k, u))

    def relay(slot):
        for step, k, u in relays[slot]:
            step(k, u)

    loads["grid"].wait()
    frames, height, across = grid_ref[0, 0], grid_ref[0, 1], grid_ref[0, 2]
    length = frames * height * across
    for d in range(n_seq):
        source = lax.rem(me_s + n_seq - d, n_seq)
        fill_tables(cos_buf, sin_buf, d * rows, rows, source * rows, (height, across))
    is_even = lax.broadcasted_iota(jnp.int32, (1, HEAD_DIM), 1) % 2 == 0
    key_slot = lax.broadcasted_iota(jnp.int32, (1, total), 1)
    slot = key_slot // rows
    source = lax.rem(me_s + n_seq - slot, n_seq)
    live_keys = source * rows + key_slot % rows < length
    factor = math.log2(math.e) / math.sqrt(HEAD_DIM)

    for name in ("head_w", "bias", "gate", "mod", "hidden", "w"):
        loads[name].wait()
    channels = head_w.shape[0]
    on_diag = lax.broadcasted_iota(jnp.int32, (channels, channels), 0) == lax.broadcasted_iota(
        jnp.int32, (channels, channels), 1
    )
    bias_col[...] = jnp.broadcast_to(
        jnp.sum(jnp.where(on_diag, bias_ref[...], 0.0), axis=1, keepdims=True), bias_col.shape
    )
    drain(qkv_buf.at[:, 0:rows, :], load_sem.at[1])

    pieces = rows // tail_rows

    def o_copy(d, j):
        cols = slice(j * HEAD_DIM, (j + 1) * HEAD_DIM)
        back = n_seq - d
        return remote(
            o_buf.at[(d - 1) * rows : d * rows, cols],
            att_buf.at[back * rows : (back + 1) * rows, cols],
            o_send, o_recv.at[back - 1, j], seq=lax.rem(me_s + back, n_seq),
        )

    def tail_copy(d, t):
        cols = slice((heads - 1) * HEAD_DIM, heads * HEAD_DIM)
        back = n_seq - d
        first = (d - 1) * rows + t * tail_rows
        there = back * rows + t * tail_rows
        return remote(
            o_buf.at[first : first + tail_rows, cols],
            att_buf.at[there : there + tail_rows, cols],
            o_send, o_recv.at[back - 1, heads - 1 + t], seq=lax.rem(me_s + back, n_seq),
        )

    def attend(j, d, last_head):
        cols = slice(j * HEAD_DIM, (j + 1) * HEAD_DIM)
        part = slice(d * rows, (d + 1) * rows)
        rot_q = rotate(qkv_buf[1, part, cols], cos_buf[part, :], sin_buf[part, :], is_even)
        scores = lax.dot_general(
            rot_q, rot_buf[...], (((1,), (1,)), ((), ())), preferred_element_type=jnp.float32
        )
        scores = jnp.where(live_keys, scores, masked_score)
        top = jnp.max(scores, axis=-1, keepdims=True)
        weights = jnp.exp2((scores - top) * factor)
        weight_sum = jnp.sum(weights, axis=-1, keepdims=True)
        mixed = jnp.dot(
            weights.astype(jnp.bfloat16), qkv_buf[2, :, cols], preferred_element_type=jnp.float32
        )
        out = (mixed / weight_sum).astype(jnp.bfloat16)
        if d == 0:
            att_buf[part, cols] = out
            return
        o_buf[(d - 1) * rows : d * rows, cols] = out
        if last_head:
            for t in range(pieces):
                tail_copy(d, t).start()
        else:
            o_copy(d, j).start()

    relay(-1)
    for j in range(heads):
        cols = slice(j * HEAD_DIM, (j + 1) * HEAD_DIM)
        for d in range(1, n_seq):
            drain(qkv_buf.at[:, d * rows : (d + 1) * rows, cols], in_recv.at[d - 1, j])
        rot_buf[...] = rotate(qkv_buf[0, :, cols], cos_buf[...], sin_buf[...], is_even)
        for i, d in enumerate((*range(1, n_seq), 0)):
            attend(j, d, j == heads - 1)
            relay(j * n_seq + i)

    finish_gather()

    def w_rows(owner, j, count):
        start = pl.multiple_of(owner * group + j * HEAD_DIM, HEAD_DIM)
        return w_buf[pl.ds(start, count * HEAD_DIM), :]

    proj_buf[...] = hid_buf[...].astype(jnp.float32) + gate_ref[...] * jnp.dot(
        att_buf[0:rows, :], w_rows(me_s, 0, heads), preferred_element_type=jnp.float32
    )
    last_d = n_seq - 1
    for j in range(heads):
        for d in range(1, n_seq):
            if j == heads - 1:
                if d == last_d:
                    continue
                for t in range(pieces):
                    tail_copy(n_seq - d, t).wait_recv()
            else:
                o_copy(n_seq - d, j).wait_recv()
            owner = lax.rem(me_s + n_seq - d, n_seq)
            proj_buf[...] += gate_ref[...] * jnp.dot(
                att_buf[d * rows : (d + 1) * rows, j * HEAD_DIM : (j + 1) * HEAD_DIM],
                w_rows(owner, j, 1),
                preferred_element_type=jnp.float32,
            )

    own_width = channels // 2
    own_chan = pl.ds(pl.multiple_of(me_c * own_width, own_width), own_width)
    other_chan = pl.ds(pl.multiple_of(other * own_width, own_width), own_width)
    swap_rows = max(tail_rows, LANES)
    swaps = [
        remote(
            pred_buf.at[other_chan, s * swap_rows : (s + 1) * swap_rows],
            other_buf.at[:, s * swap_rows : (s + 1) * swap_rows],
            p_send, p_recv.at[s], cfg=other,
        )
        for s in range(rows // swap_rows)
    ]
    owner = lax.rem(me_s + n_seq - last_d, n_seq)
    last_cols = slice((heads - 1) * HEAD_DIM, heads * HEAD_DIM)
    for t in range(pieces):
        tail_copy(n_seq - last_d, t).wait_recv()
        part = slice(t * tail_rows, (t + 1) * tail_rows)
        first = last_d * rows + t * tail_rows
        mixed = proj_buf[part, :] + gate_ref[...] * jnp.dot(
            att_buf[first : first + tail_rows, last_cols],
            w_rows(owner, heads - 1, 1),
            preferred_element_type=jnp.float32,
        )
        average = jnp.mean(mixed, axis=-1, keepdims=True)
        centered = mixed - average
        spread_sq = jnp.mean(centered * centered, axis=-1, keepdims=True)
        normed = centered * lax.rsqrt(spread_sq + norm_eps)
        modded = (normed * (1.0 + mod_ref[1:2, :]) + mod_ref[0:1, :]).astype(jnp.bfloat16)
        pred_buf[:, part] = (
            lax.dot_general(
                head_w[...], modded, (((1,), (1,)), ((), ())), preferred_element_type=jnp.float32
            )
            + bias_col[:, 0:tail_rows]
        )
        if (t + 1) * tail_rows % swap_rows == 0:
            swaps[(t + 1) * tail_rows // swap_rows - 1].start()

    live = me_s * rows + lax.broadcasted_iota(jnp.int32, (own_width, rows), 1) < length

    drain(qkv_buf.at[:, rows:total, :], in_send)
    drain(o_buf, o_send)
    at_end = jnp.logical_or(place == 0, place == line_len - 1)

    @pl.when(at_end)
    def _():
        drain(w_buf.at[0 : 3 * line_len * half, :], w_send)

    @pl.when(jnp.logical_not(at_end))
    def _():
        drain(w_buf, w_send)

    is_cond = me_c == 0
    for s, swap in enumerate(swaps):
        part = slice(s * swap_rows, (s + 1) * swap_rows)
        swap.wait_recv()
        own_cols, other_cols = pred_buf[own_chan, part], other_buf[:, part]
        cond = jnp.where(is_cond, own_cols, other_cols)
        uncond = jnp.where(is_cond, other_cols, own_cols)
        base_ref[:, part] = jnp.where(live[:, part], uncond, 0.0)
        gain_ref[:, part] = jnp.where(live[:, part], cond - uncond, 0.0)
    drain(pred_buf.at[own_chan, :], p_send)


def solution(mesh):
    n_seq, n_req = mesh.shape["seq"], mesh.shape["req"]

    def on_device(
        queries,
        key_vectors,
        values,
        hidden,
        out_proj,
        head_weight,
        head_bias,
        attn_gate,
        shift_scale,
        grid_shape,
        step_index,
        guide_scale,
        latent,
    ):
        rows, width = queries.shape[2:]
        model = hidden.shape[3]
        channels = head_weight.shape[1]
        own_width = latent.shape[2]
        group = width // n_seq
        heads = group // HEAD_DIM
        line_len = n_req // 2
        total = n_seq * rows
        half = out_proj.shape[0] // 2
        subs = 2 if half % 32 == 0 else 1
        tail_rows = 128
        pieces = rows // tail_rows
        swaps = rows // max(tail_rows, LANES)
        hbm = pl.BlockSpec(memory_space=pltpu.HBM)
        dma = pltpu.SemaphoreType.DMA
        base, gain = pl.pallas_call(
            functools.partial(kernel, n_seq, n_req, tail_rows),
            out_shape=(pltpu.VMEM((own_width, rows), jnp.float32), pltpu.VMEM((own_width, rows), jnp.float32)),
            in_specs=[hbm] * 10,
            out_specs=(pl.BlockSpec(memory_space=pltpu.VMEM), pl.BlockSpec(memory_space=pltpu.VMEM)),
            scratch_shapes=[
                pltpu.VMEM((3, total, group), jnp.bfloat16),
                pltpu.VMEM((total, HEAD_DIM), jnp.bfloat16),
                pltpu.VMEM((total - rows, group), jnp.bfloat16),
                pltpu.VMEM((total, group), jnp.bfloat16),
                pltpu.VMEM((rows, model), jnp.bfloat16),
                pltpu.VMEM((width, model), jnp.bfloat16),
                pltpu.VMEM((total, HEAD_DIM), jnp.float32),
                pltpu.VMEM((total, HEAD_DIM), jnp.float32),
                pltpu.VMEM((channels, rows), jnp.float32),
                pltpu.VMEM((own_width, rows), jnp.float32),
                pltpu.VMEM((rows, model), jnp.float32),
                pltpu.VMEM((channels, model), jnp.bfloat16),
                pltpu.VMEM((1, channels), jnp.float32),
                pltpu.VMEM((channels, LANES), jnp.float32),
                pltpu.VMEM((1, model), jnp.float32),
                pltpu.VMEM((2, model), jnp.float32),
                pltpu.SMEM((1, 3), jnp.int32),
                dma((8,)),
                pltpu.SemaphoreType.REGULAR((3,)),
                dma(()),
                dma((n_seq - 1, heads)),
                dma(()),
                dma((n_seq - 1, heads - 1 + pieces)),
                dma(()),
                dma((line_len, subs)),
                dma((line_len, subs)),
                dma(()),
                dma(()),
                dma((swaps,)),
            ],
            compiler_params=pltpu.CompilerParams(
                collective_id=0, has_side_effects=True, vmem_limit_bytes=56 * 1024 * 1024
            ),
        )(
            queries[0, 0],
            key_vectors[0, 0],
            values[0, 0],
            hidden[0, 0],
            out_proj,
            head_weight.T,
            head_bias[None, :],
            attn_gate,
            shift_scale[0],
            grid_shape,
        )
        step_value = step_index[0].astype(jnp.float32)
        delta = noise_level(step_value + 1.0) - noise_level(step_value)
        velocity = base + guide_scale[0] * gain
        next_latent = latent[0].T + delta * velocity
        return (next_latent.T[None], velocity.T[None])

    return jax.shard_map(
        on_device,
        mesh=mesh,
        in_specs=(
            P("req", "cfg", "seq", None),
            P("req", "cfg", "seq", None),
            P("req", "cfg", "seq", None),
            P("req", "cfg", "seq", None),
            P("req", None),
            P(),
            P(),
            P("req", None),
            P("req", None, None),
            P("req", None),
            P("req"),
            P("req"),
            P("req", "seq", "cfg"),
        ),
        out_specs=(P("req", "seq", "cfg"), P("req", "seq", "cfg")),
        check_vma=False,
    )
```

```python
import functools
import math

import jax
import jax.numpy as jnp
from jax import lax
from jax.experimental import pallas as pl
from jax.experimental.pallas import tpu as pltpu
from jax.sharding import PartitionSpec as P

HEAD_DIM = 128
STEPS = 20
LANES = 128
COLS = 256
BLOCK = 32

masked_score = -1e30
norm_eps = 1e-06
shift_factor = 5.0
MESH = pl.DeviceIdType.MESH


def noise_level(step_value):
    progress = 1.0 - step_value / STEPS
    return shift_factor * progress / (1.0 + (shift_factor - 1.0) * progress)


def fill_tables(cos_ref, sin_ref, start, rows, first_token, dims):
    height, width = dims
    sixth = HEAD_DIM // 6
    time_pairs = (HEAD_DIM - 4 * sixth) // 2
    lane = lax.broadcasted_iota(jnp.int32, (8, HEAD_DIM), 1)
    pair = lane // 2
    is_time = pair < time_pairs
    is_row = pair < time_pairs + sixth
    pair_f = pair.astype(jnp.float32)
    space = pair_f - time_pairs
    exponent = jnp.where(
        is_time, pair_f / time_pairs, jnp.where(is_row, space / sixth, (space - sixth) / sixth)
    )
    freq = jnp.exp(exponent * -math.log(10000.0))[0:1]
    sign = jnp.where(lane % 2 == 0, -1.0, 1.0).astype(jnp.float32)[0:1]
    lanes = lax.broadcasted_iota(jnp.int32, (rows, HEAD_DIM), 1) // 2
    token = (first_token + lax.broadcasted_iota(jnp.int32, (rows, HEAD_DIM), 0)).astype(jnp.float32)
    h_vec = jnp.full((rows, HEAD_DIM), height.astype(jnp.float32))
    w_vec = jnp.full((rows, HEAD_DIM), width.astype(jnp.float32))
    frame = jnp.floor((token + 0.5) / (h_vec * w_vec))
    line = jnp.floor((token + 0.5) / w_vec)
    row = line - h_vec * jnp.floor((line + 0.5) / h_vec)
    col = token - w_vec * line
    position = jnp.where(lanes < time_pairs, frame, jnp.where(lanes < time_pairs + sixth, row, col))
    angles = position * freq
    cos_ref[start : start + rows, :] = jnp.cos(angles)
    sin_ref[start : start + rows, :] = jnp.sin(angles) * sign


def rotate(x, cos, sin, is_even):
    source = x.astype(jnp.float32)
    partner = jnp.where(
        is_even, pltpu.roll(source, HEAD_DIM - 1, 1), pltpu.roll(source, 1, 1)
    )
    return (source * cos + partner * sin).astype(jnp.bfloat16)


def kernel(
    n_seq,
    n_req,
    tail_rows,
    q_hbm,
    k_hbm,
    v_hbm,
    hidden_hbm,
    w_hbm,
    head_w_hbm,
    bias_hbm,
    gate_hbm,
    mod_hbm,
    grid_hbm,
    base_ref,
    gain_ref,
    qkv_buf,
    rot_buf,
    o_buf,
    att_buf,
    hid_buf,
    w_buf,
    cos_buf,
    sin_buf,
    pred_buf,
    other_buf,
    proj_buf,
    head_w,
    bias_ref,
    const_col,
    rhs_buf,
    tail_mat,
    base_prod,
    base_sum,
    base_buf,
    gate_ref,
    mod_ref,
    grid_ref,
    load_sem,
    ready_sem,
    in_send,
    in_recv,
    o_send,
    o_recv,
    w_send,
    line_recv,
    x_recv,
    c_recv,
    p_send,
    p_recv,
):
    rows = hid_buf.shape[0]
    group = qkv_buf.shape[2]
    heads = group // HEAD_DIM
    total = n_seq * rows
    shard = w_hbm.shape[0]
    half = shard // 2
    subs = line_recv.shape[1]
    sub = half // subs
    line_len = n_req // 2
    me_s = lax.axis_index("seq")
    me_c = lax.axis_index("cfg")
    me_r = lax.axis_index("req")
    place = me_r // 2
    side_x = me_r % 2
    x_mate = me_r + 1 - 2 * side_x
    other = 1 - me_c
    below, above = jnp.maximum(me_r - 2, 0), jnp.minimum(me_r + 2, n_req - 1)
    has_below, has_above = place >= 1, place <= line_len - 2

    def remote(src, dst, s_sem, r_sem, **target):
        return pltpu.make_async_remote_copy(
            src_ref=src, dst_ref=dst, send_sem=s_sem, recv_sem=r_sem,
            device_id=target, device_id_type=MESH,
        )

    def drain(ref, sem):
        pltpu.make_async_copy(ref, ref, sem).wait()

    def signal(sem, **target):
        pl.semaphore_signal(sem, inc=1, device_id=target, device_id_type=MESH)

    barrier = pltpu.get_barrier_semaphore()
    for d in range(1, n_seq):
        signal(barrier, seq=lax.rem(me_s + d, n_seq))

    @pl.when(me_c == 0)
    def _():
        signal(barrier, cfg=other)

    @pl.when(has_above)
    def _():
        signal(barrier, req=above)

    @pl.when(side_x == 0)
    def _():
        signal(barrier, req=x_mate)

    def head_cols(owner, j):
        return pl.ds(pl.multiple_of(owner * group + j * HEAD_DIM, HEAD_DIM), HEAD_DIM)

    own_group = pl.ds(pl.multiple_of(me_s * group, group), group)
    loads = {
        "grid": pltpu.make_async_copy(grid_hbm, grid_ref, load_sem.at[0]),
        "k": pltpu.make_async_copy(k_hbm.at[:, own_group], qkv_buf.at[0, 0:rows, :], load_sem.at[1]),
        "q": pltpu.make_async_copy(q_hbm.at[:, own_group], qkv_buf.at[1, 0:rows, :], load_sem.at[1]),
        "v": pltpu.make_async_copy(v_hbm.at[:, own_group], qkv_buf.at[2, 0:rows, :], load_sem.at[1]),
        "w": pltpu.make_async_copy(
            w_hbm, w_buf.at[pl.ds(pl.multiple_of(me_r * shard, shard), shard), :], load_sem.at[2]
        ),
        "hidden": pltpu.make_async_copy(hidden_hbm, hid_buf, load_sem.at[3]),
        "head_w": pltpu.make_async_copy(head_w_hbm, head_w, load_sem.at[4]),
        "bias": pltpu.make_async_copy(bias_hbm, bias_ref, load_sem.at[5]),
        "gate": pltpu.make_async_copy(gate_hbm, gate_ref, load_sem.at[6]),
        "mod": pltpu.make_async_copy(mod_hbm, mod_ref, load_sem.at[7]),
    }
    loads["grid"].start()

    pl.semaphore_wait(
        barrier,
        n_seq - 1 + me_c + side_x + jnp.where(has_below, 1, 0),
    )

    def in_copy(d, j, kind):
        owner = lax.rem(me_s + d, n_seq)
        src = (k_hbm, q_hbm, v_hbm)[kind].at[:, head_cols(owner, j)]
        dst = qkv_buf.at[kind, d * rows : (d + 1) * rows, j * HEAD_DIM : (j + 1) * HEAD_DIM]
        return remote(src, dst, in_send, in_recv.at[d - 1, j], seq=owner)

    for j in range(heads):
        for d in range(1, n_seq):
            for kind in range(3):
                in_copy(d, j, kind).start()

    @pl.when(me_c == 1)
    def _():
        signal(ready_sem.at[0], cfg=other)

    @pl.when(has_below)
    def _():
        signal(ready_sem.at[1], req=below)

    @pl.when(side_x == 1)
    def _():
        signal(ready_sem.at[2], req=x_mate)

    for name, load in loads.items():
        if name != "grid":
            load.start()

    def piece(owner, which, u):
        start = pl.multiple_of(owner * shard + which * half + u * sub, sub)
        return w_buf.at[pl.ds(start, sub), :]

    def own_src(u):
        return w_hbm.at[pl.ds(pl.multiple_of(me_c * half + u * sub, sub), sub), :]

    def toward(side):
        return below if side == 0 else above

    def can_pass(side):
        return has_below if side == 0 else has_above

    def comes(side, k):
        return place + k <= line_len - 1 if side == 0 else place - k >= 0

    def owner_of(base, side, k):
        return base + 2 * k if side == 0 else base - 2 * k

    def line_copy(src, owner, side, u):
        return remote(src, piece(owner, me_c, u), w_send, line_recv.at[owner // 2, u], req=toward(side))

    def x_copy(src, owner, u):
        return remote(src, piece(owner, me_c, u), w_send, x_recv.at[owner // 2, u], req=x_mate)

    def c_copy(owner, u):
        return remote(
            piece(owner, me_c, u), piece(owner, me_c, u), w_send, c_recv.at[owner // 2], cfg=other
        )

    @pl.when(has_above)
    def _():
        pl.semaphore_wait(ready_sem.at[1], 1)

    for u in range(subs):
        for side in range(2):
            @pl.when(can_pass(side))
            def _():
                line_copy(own_src(u), me_r, side, u).start()

    @pl.when(side_x == 0)
    def _():
        pl.semaphore_wait(ready_sem.at[2], 1)

    for u in range(subs):
        x_copy(own_src(u), me_r, u).start()

    @pl.when(me_c == 0)
    def _():
        pl.semaphore_wait(ready_sem.at[0], 1)

    def line_step(k, u):
        for side in range(2):
            @pl.when(comes(side, k))
            def _():
                owner = owner_of(me_r, side, k)
                line_copy(piece(owner, me_c, u), owner, side, u).wait_recv()
                if k < line_len - 1:
                    @pl.when(can_pass(side))
                    def _():
                        line_copy(piece(owner, me_c, u), owner, side, u).start()
                x_copy(piece(owner, me_c, u), owner, u).start()
                c_copy(owner, u).start()

    farthest = jnp.maximum(place, line_len - 1 - place)

    def x_step(k, u, last=False):
        for side in range(2 if k else 1):
            ready = k == farthest if last else k < farthest
            @pl.when(jnp.logical_and(comes(side, k), ready))
            def _():
                owner = owner_of(x_mate, side, k)
                x_copy(piece(owner, me_c, u), owner, u).wait_recv()
                c_copy(owner, u).start()

    def wait_place(spot):
        @pl.when(spot == place)
        def _():
            drain(w_buf.at[0:half, :], c_recv.at[spot])

        @pl.when(spot != place)
        def _():
            drain(w_buf.at[0:shard, :], c_recv.at[spot])

    slots = heads * n_seq
    relays = {slot: [] for slot in range(-1, slots)}
    line_steps = [(k, u) for k in range(1, line_len) for u in range(subs)]
    x_steps = [(k, u) for k in range(line_len) for u in range(subs)]
    for i, (k, u) in enumerate(line_steps):
        relays[i * (5 * slots // 8) // len(line_steps) - 1].append((line_step, k, u))
    for i, (k, u) in enumerate(x_steps):
        relays[i * slots // len(x_steps)].append((x_step, k, u))

    def relay(slot):
        for step, k, u in relays[slot]:
            step(k, u)

    loads["grid"].wait()
    frames, height, across = grid_ref[0, 0], grid_ref[0, 1], grid_ref[0, 2]
    length = frames * height * across
    for d in range(n_seq):
        source = lax.rem(me_s + n_seq - d, n_seq)
        fill_tables(cos_buf, sin_buf, d * rows, rows, source * rows, (height, across))
    is_even = lax.broadcasted_iota(jnp.int32, (1, HEAD_DIM), 1) % 2 == 0
    key_slot = lax.broadcasted_iota(jnp.int32, (1, total), 1)
    slot = key_slot // rows
    source = lax.rem(me_s + n_seq - slot, n_seq)
    live_keys = source * rows + key_slot % rows < length
    factor = math.log2(math.e) / math.sqrt(HEAD_DIM)

    for name in ("head_w", "bias", "gate", "mod", "hidden", "w"):
        loads[name].wait()
    channels = head_w.shape[0]
    on_diag = lax.broadcasted_iota(jnp.int32, (channels, channels), 0) == lax.broadcasted_iota(
        jnp.int32, (channels, channels), 1
    )
    bias = jnp.sum(jnp.where(on_diag, bias_ref[...], 0.0), axis=1, keepdims=True)
    shift = mod_ref[0:1, :]
    shift_top = shift.astype(jnp.bfloat16)
    shift_rest = (shift - shift_top.astype(jnp.float32)).astype(jnp.bfloat16)
    shift_head = sum(
        lax.dot_general(
            head_w[...], jnp.broadcast_to(term, (8, term.shape[1])), (((1,), (1,)), ((), ())),
            preferred_element_type=jnp.float32,
        )[:, 0:1]
        for term in (shift_top, shift_rest)
    )
    const_col[...] = jnp.broadcast_to(shift_head + bias, const_col.shape)
    scaled_head = head_w[...].astype(jnp.float32) * (1.0 + mod_ref[1:2, :])
    head_top = scaled_head.astype(jnp.bfloat16)
    rhs_buf[0:channels, :] = head_top
    rhs_buf[channels : 2 * channels, :] = (
        scaled_head - head_top.astype(jnp.float32)
    ).astype(jnp.bfloat16)
    drain(qkv_buf.at[:, 0:rows, :], load_sem.at[1])

    pieces = rows // tail_rows

    def o_copy(d, j):
        cols = slice(j * HEAD_DIM, (j + 1) * HEAD_DIM)
        back = n_seq - d
        return remote(
            o_buf.at[(d - 1) * rows : d * rows, cols],
            att_buf.at[back * rows : (back + 1) * rows, cols],
            o_send, o_recv.at[back - 1, j], seq=lax.rem(me_s + back, n_seq),
        )

    def tail_copy(d, t):
        cols = slice((heads - 1) * HEAD_DIM, heads * HEAD_DIM)
        back = n_seq - d
        first = (d - 1) * rows + t * tail_rows
        there = back * rows + t * tail_rows
        return remote(
            o_buf.at[first : first + tail_rows, cols],
            att_buf.at[there : there + tail_rows, cols],
            o_send, o_recv.at[back - 1, heads - 1 + t], seq=lax.rem(me_s + back, n_seq),
        )

    def attend(j, d, last_head):
        cols = slice(j * HEAD_DIM, (j + 1) * HEAD_DIM)
        part = slice(d * rows, (d + 1) * rows)
        rot_q = rotate(qkv_buf[1, part, cols], cos_buf[part, :], sin_buf[part, :], is_even)
        scores = lax.dot_general(
            rot_q, rot_buf[...], (((1,), (1,)), ((), ())), preferred_element_type=jnp.float32
        )
        scores = jnp.where(live_keys, scores, masked_score)
        top = jnp.max(scores, axis=-1, keepdims=True)
        weights = jnp.exp2((scores - top) * factor)
        weight_sum = jnp.sum(weights, axis=-1, keepdims=True)
        mixed = jnp.dot(
            weights.astype(jnp.bfloat16), qkv_buf[2, :, cols], preferred_element_type=jnp.float32
        )
        out = (mixed / weight_sum).astype(jnp.bfloat16)
        if d == 0:
            att_buf[part, cols] = out
            return
        o_buf[(d - 1) * rows : d * rows, cols] = out
        if last_head:
            for t in range(pieces):
                tail_copy(d, t).start()
        else:
            o_copy(d, j).start()

    unit = max(HEAD_DIM, 2 * shard)
    places = unit // (2 * shard)
    own_units = group // unit
    unit_heads = unit // HEAD_DIM
    last_d = n_seq - 1
    last_owner = lax.rem(me_s + n_seq - last_d, n_seq)
    split = 2 * channels
    model = hid_buf.shape[1]
    nt = (((1,), (1,)), ((), ()))

    def unit_away(owner, i):
        first = (owner * group + i * unit) // (2 * shard)
        return jnp.maximum(first + places - 1 - place, place - first)

    def unit_rows(owner, i):
        row = owner * group + i * unit
        for n in range(places):
            wait_place(row // (2 * shard) + n)
        return w_buf.at[pl.ds(pl.multiple_of(row, unit), unit), :]

    def add_unit(att, w_rows, first=False):
        for c in range(0, model, COLS):
            cols = slice(c, c + COLS)
            so_far = hid_buf[:, cols].astype(jnp.float32) if first else proj_buf[:, cols]
            proj_buf[:, cols] = so_far + gate_ref[:, cols] * jnp.dot(
                att, w_rows[:, cols], preferred_element_type=jnp.float32
            )

    def add_own(i):
        add_unit(att_buf[0:rows, i * unit : (i + 1) * unit], unit_rows(me_s, i), i == 0)

    def form_late():
        w_rows = unit_rows(last_owner, own_units - 1)
        for r in range(0, unit, BLOCK):
            gated = w_rows[r : r + BLOCK, :].astype(jnp.float32) * gate_ref[...]
            rhs_buf[split + r : split + r + BLOCK, :] = (
                gated - jnp.mean(gated, axis=-1, keepdims=True)
            ).astype(jnp.bfloat16)
        late_rows = rhs_buf[split:, :]
        late_prod = lax.dot_general(late_rows, rhs_buf[...], nt, preferred_element_type=jnp.float32)
        late_head = late_prod[:, 0:split]
        late_sum = late_head + pltpu.roll(late_head, channels, 1)
        late_top = late_sum.astype(jnp.bfloat16)
        late_rest = (late_sum - late_top.astype(jnp.float32)).astype(jnp.bfloat16)
        is_top = lax.broadcasted_iota(jnp.int32, (1, split), 1) < channels
        tail_mat[:, 0:split] = jnp.where(is_top, late_top, late_rest)
        tail_mat[:, split:] = late_prod[:, split:].astype(jnp.bfloat16)

    own_away = unit_away(me_s, 0)
    late_away = unit_away(last_owner, own_units - 1)
    own_soon = jnp.logical_and(own_away < farthest, own_units > 1)
    late_soon = jnp.logical_and(late_away < farthest, own_units > 1)
    late_last = late_away >= farthest

    relay(-1)
    for j in range(heads):
        if j == heads - 1 and j > 0:
            @pl.when(own_soon)
            def _():
                add_own(0)

            @pl.when(late_soon)
            def _():
                form_late()

        cols = slice(j * HEAD_DIM, (j + 1) * HEAD_DIM)
        for d in range(1, n_seq):
            drain(qkv_buf.at[:, d * rows : (d + 1) * rows, cols], in_recv.at[d - 1, j])
        rot_buf[...] = rotate(qkv_buf[0, :, cols], cos_buf[...], sin_buf[...], is_even)
        for i, d in enumerate((*range(1, n_seq), 0)):
            attend(j, d, j == heads - 1)
            relay(j * n_seq + i)

    for k in range(line_len // 2, line_len):
        for u in range(subs):
            x_step(k, u, True)

    @pl.when(jnp.logical_not(own_soon))
    def _():
        add_own(0)

    for i in range(1, own_units):
        add_own(i)

    @pl.when(jnp.logical_not(jnp.logical_or(late_soon, late_last)))
    def _():
        form_late()

    def wait_heads(d, i):
        for j in range(i * unit_heads, (i + 1) * unit_heads):
            if j == heads - 1:
                for t in range(pieces):
                    tail_copy(n_seq - d, t).wait_recv()
            else:
                o_copy(n_seq - d, j).wait_recv()

    for i in range(own_units):
        for d in range(1, n_seq):
            if d == last_d and i == own_units - 1:
                continue
            wait_heads(d, i)
            owner = lax.rem(me_s + n_seq - d, n_seq)
            add_unit(
                att_buf[d * rows : (d + 1) * rows, i * unit : (i + 1) * unit], unit_rows(owner, i)
            )
    for r in range(0, rows, BLOCK):
        part = slice(r, r + BLOCK)
        base = proj_buf[part, :]
        base = base - jnp.mean(base, axis=-1, keepdims=True)
        base_sum[part, :] = jnp.broadcast_to(
            jnp.sum(base * base, axis=-1, keepdims=True), (BLOCK, LANES)
        )
        base_buf[part, :] = base.astype(jnp.bfloat16)

    @pl.when(late_last)
    def _():
        form_late()

    base_prod[...] = lax.dot_general(
        base_buf[...], rhs_buf[...], nt, preferred_element_type=jnp.float32
    )

    own_width = channels // 2
    own_chan = pl.ds(pl.multiple_of(me_c * own_width, own_width), own_width)
    other_chan = pl.ds(pl.multiple_of(other * own_width, own_width), own_width)
    swap_rows = max(tail_rows, LANES)
    swaps = [
        remote(
            pred_buf.at[other_chan, s * swap_rows : (s + 1) * swap_rows],
            other_buf.at[:, s * swap_rows : (s + 1) * swap_rows],
            p_send, p_recv.at[s], cfg=other,
        )
        for s in range(rows // swap_rows)
    ]
    late_cols = slice((own_units - 1) * unit, own_units * unit)
    for j in range(heads - unit_heads, heads - 1):
        o_copy(n_seq - last_d, j).wait_recv()
    for t in range(pieces):
        tail_copy(n_seq - last_d, t).wait_recv()
        part = slice(t * tail_rows, (t + 1) * tail_rows)
        first = last_d * rows + t * tail_rows
        late_out = att_buf[first : first + tail_rows, late_cols]
        added = jnp.dot(late_out, tail_mat[...], preferred_element_type=jnp.float32)
        cross = late_out.astype(jnp.float32) * (added[:, split:] + 2.0 * base_prod[part, split:])
        square_sum = base_sum[part, 0:1] + jnp.sum(cross, axis=-1, keepdims=True)
        inverse = lax.rsqrt(jnp.maximum(square_sum, 0.0) * (1.0 / model) + norm_eps)
        turned = ((added[:, 0:split] + base_prod[part, 0:split]) * inverse).T
        pred_buf[:, part] = (
            turned[0:channels, :] + turned[channels:, :] + const_col[:, 0:tail_rows]
        )
        if (t + 1) * tail_rows % swap_rows == 0:
            swaps[(t + 1) * tail_rows // swap_rows - 1].start()

    live = me_s * rows + lax.broadcasted_iota(jnp.int32, (own_width, rows), 1) < length

    drain(qkv_buf.at[:, rows:total, :], in_send)
    drain(o_buf, o_send)
    at_end = jnp.logical_or(place == 0, place == line_len - 1)

    @pl.when(at_end)
    def _():
        drain(w_buf.at[0 : 3 * line_len * half, :], w_send)

    @pl.when(jnp.logical_not(at_end))
    def _():
        drain(w_buf, w_send)

    is_cond = me_c == 0
    for s, swap in enumerate(swaps):
        part = slice(s * swap_rows, (s + 1) * swap_rows)
        swap.wait_recv()
        own_cols, other_cols = pred_buf[own_chan, part], other_buf[:, part]
        cond = jnp.where(is_cond, own_cols, other_cols)
        uncond = jnp.where(is_cond, other_cols, own_cols)
        base_ref[:, part] = jnp.where(live[:, part], uncond, 0.0)
        gain_ref[:, part] = jnp.where(live[:, part], cond - uncond, 0.0)
    drain(pred_buf.at[own_chan, :], p_send)


def solution(mesh):
    n_seq, n_req = mesh.shape["seq"], mesh.shape["req"]

    def on_device(
        queries,
        key_vectors,
        values,
        hidden,
        out_proj,
        head_weight,
        head_bias,
        attn_gate,
        shift_scale,
        grid_shape,
        step_index,
        guide_scale,
        latent,
    ):
        rows, width = queries.shape[2:]
        model = hidden.shape[3]
        channels = head_weight.shape[1]
        own_width = latent.shape[2]
        group = width // n_seq
        heads = group // HEAD_DIM
        line_len = n_req // 2
        total = n_seq * rows
        half = out_proj.shape[0] // 2
        subs = 2 if half % 32 == 0 else 1
        tail_rows = 128
        pieces = rows // tail_rows
        swaps = rows // max(tail_rows, LANES)
        unit = max(HEAD_DIM, 2 * out_proj.shape[0])
        hbm = pl.BlockSpec(memory_space=pltpu.HBM)
        dma = pltpu.SemaphoreType.DMA
        base, gain = pl.pallas_call(
            functools.partial(kernel, n_seq, n_req, tail_rows),
            out_shape=(pltpu.VMEM((own_width, rows), jnp.float32), pltpu.VMEM((own_width, rows), jnp.float32)),
            in_specs=[hbm] * 10,
            out_specs=(pl.BlockSpec(memory_space=pltpu.VMEM), pl.BlockSpec(memory_space=pltpu.VMEM)),
            scratch_shapes=[
                pltpu.VMEM((3, total, group), jnp.bfloat16),
                pltpu.VMEM((total, HEAD_DIM), jnp.bfloat16),
                pltpu.VMEM((total - rows, group), jnp.bfloat16),
                pltpu.VMEM((total, group), jnp.bfloat16),
                pltpu.VMEM((rows, model), jnp.bfloat16),
                pltpu.VMEM((width, model), jnp.bfloat16),
                pltpu.VMEM((total, HEAD_DIM), jnp.float32),
                pltpu.VMEM((total, HEAD_DIM), jnp.float32),
                pltpu.VMEM((channels, rows), jnp.float32),
                pltpu.VMEM((own_width, rows), jnp.float32),
                pltpu.VMEM((rows, model), jnp.float32),
                pltpu.VMEM((channels, model), jnp.bfloat16),
                pltpu.VMEM((1, channels), jnp.float32),
                pltpu.VMEM((channels, LANES), jnp.float32),
                pltpu.VMEM((2 * channels + unit, model), jnp.bfloat16),
                pltpu.VMEM((unit, 2 * channels + unit), jnp.bfloat16),
                pltpu.VMEM((rows, 2 * channels + unit), jnp.float32),
                pltpu.VMEM((rows, LANES), jnp.float32),
                pltpu.VMEM((rows, model), jnp.bfloat16),
                pltpu.VMEM((1, model), jnp.float32),
                pltpu.VMEM((2, model), jnp.float32),
                pltpu.SMEM((1, 3), jnp.int32),
                dma((8,)),
                pltpu.SemaphoreType.REGULAR((3,)),
                dma(()),
                dma((n_seq - 1, heads)),
                dma(()),
                dma((n_seq - 1, heads - 1 + pieces)),
                dma(()),
                dma((line_len, subs)),
                dma((line_len, subs)),
                dma((line_len,)),
                dma(()),
                dma((swaps,)),
            ],
            compiler_params=pltpu.CompilerParams(
                collective_id=0, has_side_effects=True, vmem_limit_bytes=56 * 1024 * 1024
            ),
        )(
            queries[0, 0],
            key_vectors[0, 0],
            values[0, 0],
            hidden[0, 0],
            out_proj,
            head_weight.T,
            head_bias[None, :],
            attn_gate,
            shift_scale[0],
            grid_shape,
        )
        step_value = step_index[0].astype(jnp.float32)
        delta = noise_level(step_value + 1.0) - noise_level(step_value)
        velocity = base + guide_scale[0] * gain
        next_latent = latent[0].T + delta * velocity
        return (next_latent.T[None], velocity.T[None])

    return jax.shard_map(
        on_device,
        mesh=mesh,
        in_specs=(
            P("req", "cfg", "seq", None),
            P("req", "cfg", "seq", None),
            P("req", "cfg", "seq", None),
            P("req", "cfg", "seq", None),
            P("req", None),
            P(),
            P(),
            P("req", None),
            P("req", None, None),
            P("req", None),
            P("req"),
            P("req"),
            P("req", "seq", "cfg"),
        ),
        out_specs=(P("req", "seq", "cfg"), P("req", "seq", "cfg")),
        check_vma=False,
    )
```

```python
import functools
import math

import jax
import jax.numpy as jnp
from jax import lax
from jax.experimental import pallas as pl
from jax.experimental.pallas import tpu as pltpu
from jax.sharding import PartitionSpec as P

HEAD_DIM = 128
STEPS = 20
LANES = 128
COLS = 256
BLOCK = 32

masked_score = -1e30
norm_eps = 1e-06
shift_factor = 5.0
MESH = pl.DeviceIdType.MESH


def noise_level(step_value):
    progress = 1.0 - step_value / STEPS
    return shift_factor * progress / (1.0 + (shift_factor - 1.0) * progress)


def fill_tables(cos_ref, sin_ref, start, rows, first_token, dims):
    height, width = dims
    sixth = HEAD_DIM // 6
    time_pairs = (HEAD_DIM - 4 * sixth) // 2
    lane = lax.broadcasted_iota(jnp.int32, (8, HEAD_DIM), 1)
    pair = lane // 2
    is_time = pair < time_pairs
    is_row = pair < time_pairs + sixth
    pair_f = pair.astype(jnp.float32)
    space = pair_f - time_pairs
    exponent = jnp.where(
        is_time, pair_f / time_pairs, jnp.where(is_row, space / sixth, (space - sixth) / sixth)
    )
    freq = jnp.exp(exponent * -math.log(10000.0))[0:1]
    sign = jnp.where(lane % 2 == 0, -1.0, 1.0).astype(jnp.float32)[0:1]
    lanes = lax.broadcasted_iota(jnp.int32, (rows, HEAD_DIM), 1) // 2
    token = (first_token + lax.broadcasted_iota(jnp.int32, (rows, HEAD_DIM), 0)).astype(jnp.float32)
    h_vec = jnp.full((rows, HEAD_DIM), height.astype(jnp.float32))
    w_vec = jnp.full((rows, HEAD_DIM), width.astype(jnp.float32))
    frame = jnp.floor((token + 0.5) / (h_vec * w_vec))
    line = jnp.floor((token + 0.5) / w_vec)
    row = line - h_vec * jnp.floor((line + 0.5) / h_vec)
    col = token - w_vec * line
    position = jnp.where(lanes < time_pairs, frame, jnp.where(lanes < time_pairs + sixth, row, col))
    angles = position * freq
    cos_ref[start : start + rows, :] = jnp.cos(angles)
    sin_ref[start : start + rows, :] = jnp.sin(angles) * sign


def rotate(x, cos, sin, is_even):
    source = x.astype(jnp.float32)
    partner = jnp.where(
        is_even, pltpu.roll(source, HEAD_DIM - 1, 1), pltpu.roll(source, 1, 1)
    )
    return (source * cos + partner * sin).astype(jnp.bfloat16)


def kernel(
    n_seq,
    n_req,
    tail_rows,
    q_hbm,
    k_hbm,
    v_hbm,
    hidden_hbm,
    w_hbm,
    head_w_hbm,
    bias_hbm,
    gate_hbm,
    mod_hbm,
    grid_hbm,
    base_ref,
    gain_ref,
    qkv_buf,
    rot_buf,
    o_buf,
    att_buf,
    hid_buf,
    w_buf,
    cos_buf,
    sin_buf,
    pred_buf,
    other_buf,
    proj_buf,
    head_w,
    bias_ref,
    const_col,
    rhs_buf,
    tail_mat,
    base_prod,
    base_sum,
    sum_row,
    base_buf,
    gate_ref,
    mod_ref,
    grid_ref,
    load_sem,
    ready_sem,
    in_send,
    in_recv,
    o_send,
    o_recv,
    w_send,
    line_recv,
    x_recv,
    c_recv,
    p_send,
    p_recv,
):
    rows = hid_buf.shape[0]
    group = qkv_buf.shape[2]
    heads = group // HEAD_DIM
    total = n_seq * rows
    shard = w_hbm.shape[0]
    half = shard // 2
    subs = line_recv.shape[1]
    sub = half // subs
    line_len = n_req // 2
    me_s = lax.axis_index("seq")
    me_c = lax.axis_index("cfg")
    me_r = lax.axis_index("req")
    place = me_r // 2
    side_x = me_r % 2
    x_mate = me_r + 1 - 2 * side_x
    other = 1 - me_c
    below, above = jnp.maximum(me_r - 2, 0), jnp.minimum(me_r + 2, n_req - 1)
    has_below, has_above = place >= 1, place <= line_len - 2

    def remote(src, dst, s_sem, r_sem, **target):
        return pltpu.make_async_remote_copy(
            src_ref=src, dst_ref=dst, send_sem=s_sem, recv_sem=r_sem,
            device_id=target, device_id_type=MESH,
        )

    def drain(ref, sem):
        pltpu.make_async_copy(ref, ref, sem).wait()

    def signal(sem, **target):
        pl.semaphore_signal(sem, inc=1, device_id=target, device_id_type=MESH)

    barrier = pltpu.get_barrier_semaphore()
    for d in range(1, n_seq):
        signal(barrier, seq=lax.rem(me_s + d, n_seq))

    @pl.when(me_c == 1)
    def _():
        signal(barrier, cfg=other)

    @pl.when(has_above)
    def _():
        signal(barrier, req=above)

    @pl.when(side_x == 0)
    def _():
        signal(barrier, req=x_mate)

    def head_cols(owner, j):
        return pl.ds(pl.multiple_of(owner * group + j * HEAD_DIM, HEAD_DIM), HEAD_DIM)

    own_group = pl.ds(pl.multiple_of(me_s * group, group), group)
    loads = {
        "grid": pltpu.make_async_copy(grid_hbm, grid_ref, load_sem.at[0]),
        "k": pltpu.make_async_copy(k_hbm.at[:, own_group], qkv_buf.at[0, 0:rows, :], load_sem.at[1]),
        "q": pltpu.make_async_copy(q_hbm.at[:, own_group], qkv_buf.at[1, 0:rows, :], load_sem.at[1]),
        "v": pltpu.make_async_copy(v_hbm.at[:, own_group], qkv_buf.at[2, 0:rows, :], load_sem.at[1]),
        "w": pltpu.make_async_copy(
            w_hbm, w_buf.at[pl.ds(pl.multiple_of(me_r * shard, shard), shard), :], load_sem.at[2]
        ),
        "hidden": pltpu.make_async_copy(hidden_hbm, hid_buf, load_sem.at[3]),
        "head_w": pltpu.make_async_copy(head_w_hbm, head_w, load_sem.at[4]),
        "bias": pltpu.make_async_copy(bias_hbm, bias_ref, load_sem.at[5]),
        "gate": pltpu.make_async_copy(gate_hbm, gate_ref, load_sem.at[6]),
        "mod": pltpu.make_async_copy(mod_hbm, mod_ref, load_sem.at[7]),
    }
    loads["grid"].start()

    pl.semaphore_wait(
        barrier,
        n_seq - 1 + other + side_x + jnp.where(has_below, 1, 0),
    )

    def in_copy(d, j, kind):
        owner = lax.rem(me_s + d, n_seq)
        src = (k_hbm, q_hbm, v_hbm)[kind].at[:, head_cols(owner, j)]
        dst = qkv_buf.at[kind, d * rows : (d + 1) * rows, j * HEAD_DIM : (j + 1) * HEAD_DIM]
        return remote(src, dst, in_send, in_recv.at[d - 1, j], seq=owner)

    for j in range(heads):
        for d in range(1, n_seq):
            for kind in range(3):
                in_copy(d, j, kind).start()

    @pl.when(me_c == 0)
    def _():
        signal(ready_sem.at[0], cfg=other)

    @pl.when(has_below)
    def _():
        signal(ready_sem.at[1], req=below)

    @pl.when(side_x == 1)
    def _():
        signal(ready_sem.at[2], req=x_mate)

    for name, load in loads.items():
        if name != "grid":
            load.start()

    def piece(owner, which, u):
        start = pl.multiple_of(owner * shard + which * half + u * sub, sub)
        return w_buf.at[pl.ds(start, sub), :]

    def own_src(u):
        return w_hbm.at[pl.ds(pl.multiple_of(me_c * half + u * sub, sub), sub), :]

    def toward(side):
        return below if side == 0 else above

    def can_pass(side):
        return has_below if side == 0 else has_above

    def comes(side, k):
        return place + k <= line_len - 1 if side == 0 else place - k >= 0

    def owner_of(base, side, k):
        return base + 2 * k if side == 0 else base - 2 * k

    def line_copy(src, owner, side, u):
        return remote(src, piece(owner, me_c, u), w_send, line_recv.at[owner // 2, u], req=toward(side))

    def x_copy(src, owner, u):
        return remote(src, piece(owner, me_c, u), w_send, x_recv.at[owner // 2, u], req=x_mate)

    def c_copy(owner, u):
        return remote(
            piece(owner, me_c, u), piece(owner, me_c, u), w_send, c_recv.at[owner // 2], cfg=other
        )

    @pl.when(has_above)
    def _():
        pl.semaphore_wait(ready_sem.at[1], 1)

    for u in range(subs):
        for side in range(2):
            @pl.when(can_pass(side))
            def _():
                line_copy(own_src(u), me_r, side, u).start()

    @pl.when(side_x == 0)
    def _():
        pl.semaphore_wait(ready_sem.at[2], 1)

    for u in range(subs):
        x_copy(own_src(u), me_r, u).start()

    @pl.when(me_c == 1)
    def _():
        pl.semaphore_wait(ready_sem.at[0], 1)

    def line_step(k, u):
        for side in range(2):
            @pl.when(comes(side, k))
            def _():
                owner = owner_of(me_r, side, k)
                line_copy(piece(owner, me_c, u), owner, side, u).wait_recv()
                if k < line_len - 1:
                    @pl.when(can_pass(side))
                    def _():
                        line_copy(piece(owner, me_c, u), owner, side, u).start()
                x_copy(piece(owner, me_c, u), owner, u).start()
                c_copy(owner, u).start()

    farthest = jnp.maximum(place, line_len - 1 - place)

    def x_step(k, u, last=False):
        for side in range(2 if k else 1):
            ready = k == farthest if last else k < farthest
            @pl.when(jnp.logical_and(comes(side, k), ready))
            def _():
                owner = owner_of(x_mate, side, k)
                x_copy(piece(owner, me_c, u), owner, u).wait_recv()
                c_copy(owner, u).start()

    def wait_place(spot):
        @pl.when(spot == place)
        def _():
            drain(w_buf.at[0:half, :], c_recv.at[spot])

        @pl.when(spot != place)
        def _():
            drain(w_buf.at[0:shard, :], c_recv.at[spot])

    slots = heads * n_seq
    relays = {slot: [] for slot in range(-1, slots)}
    line_steps = [(k, u) for k in range(1, line_len) for u in range(subs)]
    x_steps = [(k, u) for k in range(line_len) for u in range(subs)]
    for i, (k, u) in enumerate(line_steps):
        relays[i * (5 * slots // 8) // len(line_steps) - 1].append((line_step, k, u))
    for i, (k, u) in enumerate(x_steps):
        relays[i * slots // len(x_steps)].append((x_step, k, u))

    def relay(slot):
        for step, k, u in relays[slot]:
            step(k, u)

    loads["grid"].wait()
    frames, height, across = grid_ref[0, 0], grid_ref[0, 1], grid_ref[0, 2]
    length = frames * height * across
    for d in range(n_seq):
        source = lax.rem(me_s + n_seq - d, n_seq)
        fill_tables(cos_buf, sin_buf, d * rows, rows, source * rows, (height, across))
    is_even = lax.broadcasted_iota(jnp.int32, (1, HEAD_DIM), 1) % 2 == 0
    key_slot = lax.broadcasted_iota(jnp.int32, (1, total), 1)
    slot = key_slot // rows
    source = lax.rem(me_s + n_seq - slot, n_seq)
    live_keys = source * rows + key_slot % rows < length
    factor = math.log2(math.e) / math.sqrt(HEAD_DIM)

    for name in ("head_w", "bias", "gate", "mod", "hidden", "w"):
        loads[name].wait()
    channels = head_w.shape[0]
    on_diag = lax.broadcasted_iota(jnp.int32, (channels, channels), 0) == lax.broadcasted_iota(
        jnp.int32, (channels, channels), 1
    )
    bias = jnp.sum(jnp.where(on_diag, bias_ref[...], 0.0), axis=1, keepdims=True)
    shift = mod_ref[0:1, :]
    shift_top = shift.astype(jnp.bfloat16)
    shift_rest = (shift - shift_top.astype(jnp.float32)).astype(jnp.bfloat16)
    shift_head = sum(
        lax.dot_general(
            head_w[...], jnp.broadcast_to(term, (8, term.shape[1])), (((1,), (1,)), ((), ())),
            preferred_element_type=jnp.float32,
        )[:, 0:1]
        for term in (shift_top, shift_rest)
    )
    const_col[...] = jnp.broadcast_to(shift_head + bias, const_col.shape)
    scaled_head = head_w[...].astype(jnp.float32) * (1.0 + mod_ref[1:2, :])
    head_top = scaled_head.astype(jnp.bfloat16)
    rhs_buf[0:channels, :] = head_top
    rhs_buf[channels : 2 * channels, :] = (
        scaled_head - head_top.astype(jnp.float32)
    ).astype(jnp.bfloat16)
    drain(qkv_buf.at[:, 0:rows, :], load_sem.at[1])

    pieces = rows // tail_rows

    def o_copy(d, j):
        cols = slice(j * HEAD_DIM, (j + 1) * HEAD_DIM)
        back = n_seq - d
        return remote(
            o_buf.at[(d - 1) * rows : d * rows, cols],
            att_buf.at[back * rows : (back + 1) * rows, cols],
            o_send, o_recv.at[back - 1, j], seq=lax.rem(me_s + back, n_seq),
        )

    def tail_copy(d, t):
        cols = slice((heads - 1) * HEAD_DIM, heads * HEAD_DIM)
        back = n_seq - d
        first = (d - 1) * rows + t * tail_rows
        there = back * rows + t * tail_rows
        return remote(
            o_buf.at[first : first + tail_rows, cols],
            att_buf.at[there : there + tail_rows, cols],
            o_send, o_recv.at[back - 1, heads - 1 + t], seq=lax.rem(me_s + back, n_seq),
        )

    def attend(j, d, last_head):
        cols = slice(j * HEAD_DIM, (j + 1) * HEAD_DIM)
        part = slice(d * rows, (d + 1) * rows)
        rot_q = rotate(qkv_buf[1, part, cols], cos_buf[part, :], sin_buf[part, :], is_even)
        scores = lax.dot_general(
            rot_q, rot_buf[...], (((1,), (1,)), ((), ())), preferred_element_type=jnp.float32
        )
        scores = jnp.where(live_keys, scores, masked_score)
        top = jnp.max(scores, axis=-1, keepdims=True)
        weights = jnp.exp2((scores - top) * factor)
        weight_sum = jnp.sum(weights, axis=-1, keepdims=True)
        mixed = jnp.dot(
            weights.astype(jnp.bfloat16), qkv_buf[2, :, cols], preferred_element_type=jnp.float32
        )
        out = (mixed / weight_sum).astype(jnp.bfloat16)
        if d == 0:
            att_buf[part, cols] = out
            return
        o_buf[(d - 1) * rows : d * rows, cols] = out
        if last_head:
            for t in range(pieces):
                tail_copy(d, t).start()
        else:
            o_copy(d, j).start()

    unit = max(HEAD_DIM, 2 * shard)
    places = unit // (2 * shard)
    own_units = group // unit
    unit_heads = unit // HEAD_DIM
    last_d = n_seq - 1
    last_owner = lax.rem(me_s + n_seq - last_d, n_seq)
    split = 2 * channels
    model = hid_buf.shape[1]
    nt = (((1,), (1,)), ((), ()))

    def unit_away(owner, i):
        first = (owner * group + i * unit) // (2 * shard)
        return jnp.maximum(first + places - 1 - place, place - first)

    def unit_rows(owner, i):
        row = owner * group + i * unit
        for n in range(places):
            wait_place(row // (2 * shard) + n)
        return w_buf.at[pl.ds(pl.multiple_of(row, unit), unit), :]

    def add_unit(att, w_rows, first=False):
        for c in range(0, model, COLS):
            cols = slice(c, c + COLS)
            so_far = hid_buf[:, cols].astype(jnp.float32) if first else proj_buf[:, cols]
            proj_buf[:, cols] = so_far + gate_ref[:, cols] * jnp.dot(
                att, w_rows[:, cols], preferred_element_type=jnp.float32
            )

    def add_own(i):
        add_unit(att_buf[0:rows, i * unit : (i + 1) * unit], unit_rows(me_s, i), i == 0)

    def form_late():
        w_rows = unit_rows(last_owner, own_units - 1)
        for r in range(0, unit, BLOCK):
            gated = w_rows[r : r + BLOCK, :].astype(jnp.float32) * gate_ref[...]
            rhs_buf[split + r : split + r + BLOCK, :] = (
                gated - jnp.mean(gated, axis=-1, keepdims=True)
            ).astype(jnp.bfloat16)
        late_rows = rhs_buf[split:, :]
        late_prod = lax.dot_general(rhs_buf[...], late_rows, nt, preferred_element_type=jnp.float32)
        late_sum = late_prod[0:channels, :] + late_prod[channels:split, :]
        late_top = late_sum.astype(jnp.bfloat16)
        tail_mat[0:channels, :] = late_top
        tail_mat[channels:split, :] = (late_sum - late_top.astype(jnp.float32)).astype(jnp.bfloat16)
        tail_mat[split:, :] = late_prod[split:, :].astype(jnp.bfloat16)

    own_away = unit_away(me_s, 0)
    late_away = unit_away(last_owner, own_units - 1)
    own_soon = jnp.logical_and(own_away < farthest, own_units > 1)
    late_soon = jnp.logical_and(late_away < farthest, own_units > 1)
    late_last = late_away >= farthest

    relay(-1)
    for j in range(heads):
        if j == heads - 1 and j > 0:
            @pl.when(own_soon)
            def _():
                add_own(0)

            @pl.when(late_soon)
            def _():
                form_late()

        cols = slice(j * HEAD_DIM, (j + 1) * HEAD_DIM)
        for d in range(1, n_seq):
            drain(qkv_buf.at[:, d * rows : (d + 1) * rows, cols], in_recv.at[d - 1, j])
        rot_buf[...] = rotate(qkv_buf[0, :, cols], cos_buf[...], sin_buf[...], is_even)
        for i, d in enumerate((*range(1, n_seq), 0)):
            attend(j, d, j == heads - 1)
            relay(j * n_seq + i)

    for k in range(line_len // 2, line_len):
        for u in range(subs):
            x_step(k, u, True)

    @pl.when(jnp.logical_not(own_soon))
    def _():
        add_own(0)

    for i in range(1, own_units):
        add_own(i)

    @pl.when(jnp.logical_not(jnp.logical_or(late_soon, late_last)))
    def _():
        form_late()

    def wait_heads(d, i):
        for j in range(i * unit_heads, (i + 1) * unit_heads):
            if j == heads - 1:
                for t in range(pieces):
                    tail_copy(n_seq - d, t).wait_recv()
            else:
                o_copy(n_seq - d, j).wait_recv()

    for i in range(own_units):
        for d in range(1, n_seq):
            if d == last_d and i == own_units - 1:
                continue
            wait_heads(d, i)
            owner = lax.rem(me_s + n_seq - d, n_seq)
            add_unit(
                att_buf[d * rows : (d + 1) * rows, i * unit : (i + 1) * unit], unit_rows(owner, i)
            )
    for r in range(0, rows, BLOCK):
        part = slice(r, r + BLOCK)
        base = proj_buf[part, :]
        base = base - jnp.mean(base, axis=-1, keepdims=True)
        base_sum[part, :] = jnp.broadcast_to(
            jnp.sum(base * base, axis=-1, keepdims=True), (BLOCK, LANES)
        )
        base_buf[part, :] = base.astype(jnp.bfloat16)
    sum_row[...] = base_sum[...].T[0:8, :]

    @pl.when(late_last)
    def _():
        form_late()

    base_prod[...] = lax.dot_general(
        rhs_buf[...], base_buf[...], nt, preferred_element_type=jnp.float32
    )

    own_width = channels // 2
    own_chan = pl.ds(pl.multiple_of(me_c * own_width, own_width), own_width)
    other_chan = pl.ds(pl.multiple_of(other * own_width, own_width), own_width)
    swap_rows = max(tail_rows, LANES)
    swaps = [
        remote(
            pred_buf.at[other_chan, s * swap_rows : (s + 1) * swap_rows],
            other_buf.at[:, s * swap_rows : (s + 1) * swap_rows],
            p_send, p_recv.at[s], cfg=other,
        )
        for s in range(rows // swap_rows)
    ]
    late_cols = slice((own_units - 1) * unit, own_units * unit)
    for j in range(heads - unit_heads, heads - 1):
        o_copy(n_seq - last_d, j).wait_recv()
    for t in range(pieces):
        tail_copy(n_seq - last_d, t).wait_recv()
        part = slice(t * tail_rows, (t + 1) * tail_rows)
        first = last_d * rows + t * tail_rows
        late_out = att_buf[first : first + tail_rows, late_cols]
        added = lax.dot_general(tail_mat[...], late_out, nt, preferred_element_type=jnp.float32)
        cross = late_out.astype(jnp.float32).T * (added[split:, :] + 2.0 * base_prod[split:, part])
        square_sum = sum_row[0:1, part] + jnp.sum(cross, axis=0, keepdims=True)
        inverse = lax.rsqrt(jnp.maximum(square_sum, 0.0) * (1.0 / model) + norm_eps)
        linear = (added[0:channels, :] + base_prod[0:channels, part]) + (
            added[channels:split, :] + base_prod[channels:split, part]
        )
        pred_buf[:, part] = linear * inverse + const_col[:, 0:tail_rows]
        if (t + 1) * tail_rows % swap_rows == 0:
            swaps[(t + 1) * tail_rows // swap_rows - 1].start()

    live = me_s * rows + lax.broadcasted_iota(jnp.int32, (own_width, rows), 1) < length

    drain(qkv_buf.at[:, rows:total, :], in_send)
    drain(o_buf, o_send)
    at_end = jnp.logical_or(place == 0, place == line_len - 1)

    @pl.when(at_end)
    def _():
        drain(w_buf.at[0 : 3 * line_len * half, :], w_send)

    @pl.when(jnp.logical_not(at_end))
    def _():
        drain(w_buf, w_send)

    is_cond = me_c == 0
    for s, swap in enumerate(swaps):
        part = slice(s * swap_rows, (s + 1) * swap_rows)
        swap.wait_recv()
        own_cols, other_cols = pred_buf[own_chan, part], other_buf[:, part]
        cond = jnp.where(is_cond, own_cols, other_cols)
        uncond = jnp.where(is_cond, other_cols, own_cols)
        base_ref[:, part] = jnp.where(live[:, part], uncond, 0.0)
        gain_ref[:, part] = jnp.where(live[:, part], cond - uncond, 0.0)
    drain(pred_buf.at[own_chan, :], p_send)


def solution(mesh):
    n_seq, n_req = mesh.shape["seq"], mesh.shape["req"]

    def on_device(
        queries,
        key_vectors,
        values,
        hidden,
        out_proj,
        head_weight,
        head_bias,
        attn_gate,
        shift_scale,
        grid_shape,
        step_index,
        guide_scale,
        latent,
    ):
        rows, width = queries.shape[2:]
        model = hidden.shape[3]
        channels = head_weight.shape[1]
        own_width = latent.shape[2]
        group = width // n_seq
        heads = group // HEAD_DIM
        line_len = n_req // 2
        total = n_seq * rows
        half = out_proj.shape[0] // 2
        subs = 2 if half % 32 == 0 else 1
        tail_rows = 128
        pieces = rows // tail_rows
        swaps = rows // max(tail_rows, LANES)
        unit = max(HEAD_DIM, 2 * out_proj.shape[0])
        hbm = pl.BlockSpec(memory_space=pltpu.HBM)
        dma = pltpu.SemaphoreType.DMA
        base, gain = pl.pallas_call(
            functools.partial(kernel, n_seq, n_req, tail_rows),
            out_shape=(pltpu.VMEM((own_width, rows), jnp.float32), pltpu.VMEM((own_width, rows), jnp.float32)),
            in_specs=[hbm] * 10,
            out_specs=(pl.BlockSpec(memory_space=pltpu.VMEM), pl.BlockSpec(memory_space=pltpu.VMEM)),
            scratch_shapes=[
                pltpu.VMEM((3, total, group), jnp.bfloat16),
                pltpu.VMEM((total, HEAD_DIM), jnp.bfloat16),
                pltpu.VMEM((total - rows, group), jnp.bfloat16),
                pltpu.VMEM((total, group), jnp.bfloat16),
                pltpu.VMEM((rows, model), jnp.bfloat16),
                pltpu.VMEM((width, model), jnp.bfloat16),
                pltpu.VMEM((total, HEAD_DIM), jnp.float32),
                pltpu.VMEM((total, HEAD_DIM), jnp.float32),
                pltpu.VMEM((channels, rows), jnp.float32),
                pltpu.VMEM((own_width, rows), jnp.float32),
                pltpu.VMEM((rows, model), jnp.float32),
                pltpu.VMEM((channels, model), jnp.bfloat16),
                pltpu.VMEM((1, channels), jnp.float32),
                pltpu.VMEM((channels, LANES), jnp.float32),
                pltpu.VMEM((2 * channels + unit, model), jnp.bfloat16),
                pltpu.VMEM((2 * channels + unit, unit), jnp.bfloat16),
                pltpu.VMEM((2 * channels + unit, rows), jnp.float32),
                pltpu.VMEM((rows, LANES), jnp.float32),
                pltpu.VMEM((8, rows), jnp.float32),
                pltpu.VMEM((rows, model), jnp.bfloat16),
                pltpu.VMEM((1, model), jnp.float32),
                pltpu.VMEM((2, model), jnp.float32),
                pltpu.SMEM((1, 3), jnp.int32),
                dma((8,)),
                pltpu.SemaphoreType.REGULAR((3,)),
                dma(()),
                dma((n_seq - 1, heads)),
                dma(()),
                dma((n_seq - 1, heads - 1 + pieces)),
                dma(()),
                dma((line_len, subs)),
                dma((line_len, subs)),
                dma((line_len,)),
                dma(()),
                dma((swaps,)),
            ],
            compiler_params=pltpu.CompilerParams(
                collective_id=0, has_side_effects=True, vmem_limit_bytes=56 * 1024 * 1024
            ),
        )(
            queries[0, 0],
            key_vectors[0, 0],
            values[0, 0],
            hidden[0, 0],
            out_proj,
            head_weight.T,
            head_bias[None, :],
            attn_gate,
            shift_scale[0],
            grid_shape,
        )
        step_value = step_index[0].astype(jnp.float32)
        delta = noise_level(step_value + 1.0) - noise_level(step_value)
        velocity = base + guide_scale[0] * gain
        next_latent = latent[0].T + delta * velocity
        return (next_latent.T[None], velocity.T[None])

    return jax.shard_map(
        on_device,
        mesh=mesh,
        in_specs=(
            P("req", "cfg", "seq", None),
            P("req", "cfg", "seq", None),
            P("req", "cfg", "seq", None),
            P("req", "cfg", "seq", None),
            P("req", None),
            P(),
            P(),
            P("req", None),
            P("req", None, None),
            P("req", None),
            P("req"),
            P("req"),
            P("req", "seq", "cfg"),
        ),
        out_specs=(P("req", "seq", "cfg"), P("req", "seq", "cfg")),
        check_vma=False,
    )
```

```python
import functools
import math

import jax
import jax.numpy as jnp
from jax import lax
from jax.experimental import pallas as pl
from jax.experimental.pallas import tpu as pltpu
from jax.sharding import PartitionSpec as P

HEAD_DIM = 128
STEPS = 20
LANES = 128
COLS = 256
BLOCK = 32

masked_score = -1e30
norm_eps = 1e-06
shift_factor = 5.0
MESH = pl.DeviceIdType.MESH


def noise_level(step_value):
    progress = 1.0 - step_value / STEPS
    return shift_factor * progress / (1.0 + (shift_factor - 1.0) * progress)


def fill_tables(cos_ref, sin_ref, start, rows, first_token, dims):
    height, width = dims
    sixth = HEAD_DIM // 6
    time_pairs = (HEAD_DIM - 4 * sixth) // 2
    lane = lax.broadcasted_iota(jnp.int32, (8, HEAD_DIM), 1)
    pair = lane // 2
    is_time = pair < time_pairs
    is_row = pair < time_pairs + sixth
    pair_f = pair.astype(jnp.float32)
    space = pair_f - time_pairs
    exponent = jnp.where(
        is_time, pair_f / time_pairs, jnp.where(is_row, space / sixth, (space - sixth) / sixth)
    )
    freq = jnp.exp(exponent * -math.log(10000.0))[0:1]
    sign = jnp.where(lane % 2 == 0, -1.0, 1.0).astype(jnp.float32)[0:1]
    lanes = lax.broadcasted_iota(jnp.int32, (rows, HEAD_DIM), 1) // 2
    token = (first_token + lax.broadcasted_iota(jnp.int32, (rows, HEAD_DIM), 0)).astype(jnp.float32)
    h_vec = jnp.full((rows, HEAD_DIM), height.astype(jnp.float32))
    w_vec = jnp.full((rows, HEAD_DIM), width.astype(jnp.float32))
    frame = jnp.floor((token + 0.5) / (h_vec * w_vec))
    line = jnp.floor((token + 0.5) / w_vec)
    row = line - h_vec * jnp.floor((line + 0.5) / h_vec)
    col = token - w_vec * line
    position = jnp.where(lanes < time_pairs, frame, jnp.where(lanes < time_pairs + sixth, row, col))
    angles = position * freq
    cos_ref[start : start + rows, :] = jnp.cos(angles)
    sin_ref[start : start + rows, :] = jnp.sin(angles) * sign


def rotate(x, cos, sin, is_even):
    source = x.astype(jnp.float32)
    partner = jnp.where(
        is_even, pltpu.roll(source, HEAD_DIM - 1, 1), pltpu.roll(source, 1, 1)
    )
    return (source * cos + partner * sin).astype(jnp.bfloat16)


def kernel(
    n_seq,
    n_req,
    tail_rows,
    q_hbm,
    k_hbm,
    v_hbm,
    hidden_hbm,
    w_hbm,
    head_w_hbm,
    bias_hbm,
    gate_hbm,
    mod_hbm,
    grid_hbm,
    base_ref,
    gain_ref,
    qkv_buf,
    rot_buf,
    o_buf,
    att_buf,
    hid_buf,
    w_buf,
    cos_buf,
    sin_buf,
    pred_buf,
    other_buf,
    proj_buf,
    head_w,
    bias_ref,
    const_col,
    rhs_buf,
    tail_mat,
    base_prod,
    base_sum,
    sum_row,
    base_buf,
    gate_ref,
    mod_ref,
    grid_ref,
    load_sem,
    ready_sem,
    in_send,
    in_recv,
    o_send,
    o_recv,
    w_send,
    line_recv,
    x_recv,
    c_recv,
    p_send,
    p_recv,
):
    rows = hid_buf.shape[0]
    group = qkv_buf.shape[2]
    heads = group // HEAD_DIM
    total = n_seq * rows
    shard = w_hbm.shape[0]
    half = shard // 2
    subs = line_recv.shape[1]
    sub = half // subs
    line_len = n_req // 2
    me_s = lax.axis_index("seq")
    me_c = lax.axis_index("cfg")
    me_r = lax.axis_index("req")
    place = me_r // 2
    side_x = me_r % 2
    x_mate = me_r + 1 - 2 * side_x
    other = 1 - me_c
    below, above = jnp.maximum(me_r - 2, 0), jnp.minimum(me_r + 2, n_req - 1)
    has_below, has_above = place >= 1, place <= line_len - 2

    def remote(src, dst, s_sem, r_sem, **target):
        return pltpu.make_async_remote_copy(
            src_ref=src, dst_ref=dst, send_sem=s_sem, recv_sem=r_sem,
            device_id=target, device_id_type=MESH,
        )

    def drain(ref, sem):
        pltpu.make_async_copy(ref, ref, sem).wait()

    def signal(sem, **target):
        pl.semaphore_signal(sem, inc=1, device_id=target, device_id_type=MESH)

    barrier = pltpu.get_barrier_semaphore()
    for d in range(1, n_seq):
        signal(barrier, seq=lax.rem(me_s + d, n_seq))

    @pl.when(me_c == 1)
    def _():
        signal(barrier, cfg=other)

    @pl.when(has_above)
    def _():
        signal(barrier, req=above)

    @pl.when(side_x == 0)
    def _():
        signal(barrier, req=x_mate)

    def head_cols(owner, j):
        return pl.ds(pl.multiple_of(owner * group + j * HEAD_DIM, HEAD_DIM), HEAD_DIM)

    own_group = pl.ds(pl.multiple_of(me_s * group, group), group)
    loads = {
        "grid": pltpu.make_async_copy(grid_hbm, grid_ref, load_sem.at[0]),
        "k": pltpu.make_async_copy(k_hbm.at[:, own_group], qkv_buf.at[0, 0:rows, :], load_sem.at[1]),
        "q": pltpu.make_async_copy(q_hbm.at[:, own_group], qkv_buf.at[1, 0:rows, :], load_sem.at[1]),
        "v": pltpu.make_async_copy(v_hbm.at[:, own_group], qkv_buf.at[2, 0:rows, :], load_sem.at[1]),
        "w": pltpu.make_async_copy(
            w_hbm, w_buf.at[pl.ds(pl.multiple_of(me_r * shard, shard), shard), :], load_sem.at[2]
        ),
        "hidden": pltpu.make_async_copy(hidden_hbm, hid_buf, load_sem.at[3]),
        "head_w": pltpu.make_async_copy(head_w_hbm, head_w, load_sem.at[4]),
        "bias": pltpu.make_async_copy(bias_hbm, bias_ref, load_sem.at[5]),
        "gate": pltpu.make_async_copy(gate_hbm, gate_ref, load_sem.at[6]),
        "mod": pltpu.make_async_copy(mod_hbm, mod_ref, load_sem.at[7]),
    }
    loads["grid"].start()

    pl.semaphore_wait(
        barrier,
        n_seq - 1 + other + side_x + jnp.where(has_below, 1, 0),
    )

    def in_copy(d, j, kind):
        owner = lax.rem(me_s + d, n_seq)
        src = (k_hbm, q_hbm, v_hbm)[kind].at[:, head_cols(owner, j)]
        dst = qkv_buf.at[kind, d * rows : (d + 1) * rows, j * HEAD_DIM : (j + 1) * HEAD_DIM]
        return remote(src, dst, in_send, in_recv.at[d - 1, j], seq=owner)

    for j in range(heads):
        for d in range(1, n_seq):
            for kind in range(3):
                in_copy(d, j, kind).start()

    @pl.when(me_c == 0)
    def _():
        signal(ready_sem.at[0], cfg=other)

    @pl.when(has_below)
    def _():
        signal(ready_sem.at[1], req=below)

    @pl.when(side_x == 1)
    def _():
        signal(ready_sem.at[2], req=x_mate)

    for name, load in loads.items():
        if name != "grid":
            load.start()

    def piece(owner, which, u):
        start = pl.multiple_of(owner * shard + which * half + u * sub, sub)
        return w_buf.at[pl.ds(start, sub), :]

    def own_src(u):
        return w_hbm.at[pl.ds(pl.multiple_of(me_c * half + u * sub, sub), sub), :]

    def toward(side):
        return below if side == 0 else above

    def can_pass(side):
        return has_below if side == 0 else has_above

    def comes(side, k):
        return place + k <= line_len - 1 if side == 0 else place - k >= 0

    def owner_of(base, side, k):
        return base + 2 * k if side == 0 else base - 2 * k

    def line_copy(src, owner, side, u):
        return remote(src, piece(owner, me_c, u), w_send, line_recv.at[owner // 2, u], req=toward(side))

    def x_copy(src, owner, u):
        return remote(src, piece(owner, me_c, u), w_send, x_recv.at[owner // 2, u], req=x_mate)

    def c_copy(owner, u):
        return remote(
            piece(owner, me_c, u), piece(owner, me_c, u), w_send, c_recv.at[owner // 2], cfg=other
        )

    @pl.when(has_above)
    def _():
        pl.semaphore_wait(ready_sem.at[1], 1)

    for u in range(subs):
        for side in range(2):
            @pl.when(can_pass(side))
            def _():
                line_copy(own_src(u), me_r, side, u).start()

    @pl.when(side_x == 0)
    def _():
        pl.semaphore_wait(ready_sem.at[2], 1)

    for u in range(subs):
        x_copy(own_src(u), me_r, u).start()

    @pl.when(me_c == 1)
    def _():
        pl.semaphore_wait(ready_sem.at[0], 1)

    def line_step(k, u):
        for side in range(2):
            @pl.when(comes(side, k))
            def _():
                owner = owner_of(me_r, side, k)
                line_copy(piece(owner, me_c, u), owner, side, u).wait_recv()
                if k < line_len - 1:
                    @pl.when(can_pass(side))
                    def _():
                        line_copy(piece(owner, me_c, u), owner, side, u).start()
                x_copy(piece(owner, me_c, u), owner, u).start()
                c_copy(owner, u).start()

    farthest = jnp.maximum(place, line_len - 1 - place)

    def x_step(k, u, last=False):
        for side in range(2 if k else 1):
            ready = k == farthest if last else k < farthest
            @pl.when(jnp.logical_and(comes(side, k), ready))
            def _():
                owner = owner_of(x_mate, side, k)
                x_copy(piece(owner, me_c, u), owner, u).wait_recv()
                c_copy(owner, u).start()

    def wait_place(spot):
        @pl.when(spot == place)
        def _():
            drain(w_buf.at[0:half, :], c_recv.at[spot])

        @pl.when(spot != place)
        def _():
            drain(w_buf.at[0:shard, :], c_recv.at[spot])

    slots = heads * n_seq
    relays = {slot: [] for slot in range(-1, slots)}
    line_steps = [(k, u) for k in range(1, line_len) for u in range(subs)]
    x_steps = [(k, u) for k in range(line_len) for u in range(subs)]
    for i, (k, u) in enumerate(line_steps):
        relays[i * (5 * slots // 8) // len(line_steps) - 1].append((line_step, k, u))
    for i, (k, u) in enumerate(x_steps):
        relays[i * slots // len(x_steps)].append((x_step, k, u))

    def relay(slot):
        for step, k, u in relays[slot]:
            step(k, u)

    loads["grid"].wait()
    frames, height, across = grid_ref[0, 0], grid_ref[0, 1], grid_ref[0, 2]
    length = frames * height * across
    for d in range(n_seq):
        source = lax.rem(me_s + n_seq - d, n_seq)
        fill_tables(cos_buf, sin_buf, d * rows, rows, source * rows, (height, across))
    is_even = lax.broadcasted_iota(jnp.int32, (1, HEAD_DIM), 1) % 2 == 0
    key_slot = lax.broadcasted_iota(jnp.int32, (1, total), 1)
    slot = key_slot // rows
    source = lax.rem(me_s + n_seq - slot, n_seq)
    live_keys = source * rows + key_slot % rows < length
    factor = math.log2(math.e) / math.sqrt(HEAD_DIM)

    for name in ("head_w", "bias", "gate", "mod", "hidden", "w"):
        loads[name].wait()
    channels = head_w.shape[0]
    on_diag = lax.broadcasted_iota(jnp.int32, (channels, channels), 0) == lax.broadcasted_iota(
        jnp.int32, (channels, channels), 1
    )
    bias = jnp.sum(jnp.where(on_diag, bias_ref[...], 0.0), axis=1, keepdims=True)
    shift = mod_ref[0:1, :]
    shift_top = shift.astype(jnp.bfloat16)
    shift_rest = (shift - shift_top.astype(jnp.float32)).astype(jnp.bfloat16)
    shift_head = sum(
        lax.dot_general(
            head_w[...], jnp.broadcast_to(term, (8, term.shape[1])), (((1,), (1,)), ((), ())),
            preferred_element_type=jnp.float32,
        )[:, 0:1]
        for term in (shift_top, shift_rest)
    )
    const_col[...] = jnp.broadcast_to(shift_head + bias, const_col.shape)
    scaled_head = head_w[...].astype(jnp.float32) * (1.0 + mod_ref[1:2, :])
    head_top = scaled_head.astype(jnp.bfloat16)
    rhs_buf[0:channels, :] = head_top
    rhs_buf[channels : 2 * channels, :] = (
        scaled_head - head_top.astype(jnp.float32)
    ).astype(jnp.bfloat16)
    drain(qkv_buf.at[:, 0:rows, :], load_sem.at[1])

    pieces = rows // tail_rows

    def o_copy(d, j):
        cols = slice(j * HEAD_DIM, (j + 1) * HEAD_DIM)
        back = n_seq - d
        return remote(
            o_buf.at[(d - 1) * rows : d * rows, cols],
            att_buf.at[back * rows : (back + 1) * rows, cols],
            o_send, o_recv.at[back - 1, j], seq=lax.rem(me_s + back, n_seq),
        )

    def tail_copy(d, t):
        cols = slice((heads - 1) * HEAD_DIM, heads * HEAD_DIM)
        back = n_seq - d
        first = (d - 1) * rows + t * tail_rows
        there = back * rows + t * tail_rows
        return remote(
            o_buf.at[first : first + tail_rows, cols],
            att_buf.at[there : there + tail_rows, cols],
            o_send, o_recv.at[back - 1, heads - 1 + t], seq=lax.rem(me_s + back, n_seq),
        )

    def attend(j, d, last_head):
        cols = slice(j * HEAD_DIM, (j + 1) * HEAD_DIM)
        part = slice(d * rows, (d + 1) * rows)
        rot_q = rotate(qkv_buf[1, part, cols], cos_buf[part, :], sin_buf[part, :], is_even)
        scores = lax.dot_general(
            rot_q, rot_buf[...], (((1,), (1,)), ((), ())), preferred_element_type=jnp.float32
        )
        scores = jnp.where(live_keys, scores, masked_score)
        top = jnp.max(scores, axis=-1, keepdims=True)
        weights = jnp.exp2((scores - top) * factor)
        weight_sum = jnp.sum(weights, axis=-1, keepdims=True)
        mixed = jnp.dot(
            weights.astype(jnp.bfloat16), qkv_buf[2, :, cols], preferred_element_type=jnp.float32
        )
        out = (mixed / weight_sum).astype(jnp.bfloat16)
        if d == 0:
            att_buf[part, cols] = out
            return
        o_buf[(d - 1) * rows : d * rows, cols] = out
        if last_head:
            for t in range(pieces):
                tail_copy(d, t).start()
        else:
            o_copy(d, j).start()

    unit = max(HEAD_DIM, 2 * shard)
    places = unit // (2 * shard)
    own_units = group // unit
    unit_heads = unit // HEAD_DIM
    last_d = n_seq - 1
    last_owner = lax.rem(me_s + n_seq - last_d, n_seq)
    split = 2 * channels
    model = hid_buf.shape[1]
    nt = (((1,), (1,)), ((), ()))

    def unit_away(owner, i):
        first = (owner * group + i * unit) // (2 * shard)
        return jnp.maximum(first + places - 1 - place, place - first)

    def unit_rows(owner, i):
        row = owner * group + i * unit
        for n in range(places):
            wait_place(row // (2 * shard) + n)
        return w_buf.at[pl.ds(pl.multiple_of(row, unit), unit), :]

    def add_unit(att, w_rows, first=False):
        for c in range(0, model, COLS):
            cols = slice(c, c + COLS)
            so_far = hid_buf[:, cols].astype(jnp.float32) if first else proj_buf[:, cols]
            proj_buf[:, cols] = so_far + gate_ref[:, cols] * jnp.dot(
                att, w_rows[:, cols], preferred_element_type=jnp.float32
            )

    def add_own(i):
        add_unit(att_buf[0:rows, i * unit : (i + 1) * unit], unit_rows(me_s, i), i == 0)

    def form_late():
        w_rows = unit_rows(last_owner, own_units - 1)
        for r in range(0, unit, BLOCK):
            gated = w_rows[r : r + BLOCK, :].astype(jnp.float32) * gate_ref[...]
            rhs_buf[split + r : split + r + BLOCK, :] = (
                gated - jnp.mean(gated, axis=-1, keepdims=True)
            ).astype(jnp.bfloat16)
        late_rows = rhs_buf[split:, :]
        late_prod = lax.dot_general(rhs_buf[...], late_rows, nt, preferred_element_type=jnp.float32)
        late_sum = late_prod[0:channels, :] + late_prod[channels:split, :]
        late_top = late_sum.astype(jnp.bfloat16)
        tail_mat[0:channels, :] = late_top
        tail_mat[channels:split, :] = (late_sum - late_top.astype(jnp.float32)).astype(jnp.bfloat16)
        tail_mat[split:, :] = late_prod[split:, :].astype(jnp.bfloat16)

    own_away = unit_away(me_s, 0)
    late_away = unit_away(last_owner, own_units - 1)
    own_soon = jnp.logical_and(own_away < farthest, own_units > 1)
    late_soon = jnp.logical_and(late_away < farthest, own_units > 1)
    late_last = late_away >= farthest

    relay(-1)
    for j in range(heads):
        if j == heads - 1 and j > 0:
            @pl.when(own_soon)
            def _():
                add_own(0)

            @pl.when(late_soon)
            def _():
                form_late()

        cols = slice(j * HEAD_DIM, (j + 1) * HEAD_DIM)
        for d in range(1, n_seq):
            drain(qkv_buf.at[:, d * rows : (d + 1) * rows, cols], in_recv.at[d - 1, j])
        rot_buf[...] = rotate(qkv_buf[0, :, cols], cos_buf[...], sin_buf[...], is_even)
        for i, d in enumerate((*range(1, n_seq), 0)):
            attend(j, d, j == heads - 1)
            relay(j * n_seq + i)

    def last_relays():
        for k in range(line_len // 2, line_len):
            for u in range(subs):
                x_step(k, u, True)

    own_far = jnp.maximum(own_away, unit_away(me_s, own_units - 1)) >= farthest

    @pl.when(own_far)
    def _():
        last_relays()

    @pl.when(jnp.logical_not(own_soon))
    def _():
        add_own(0)

    for i in range(1, own_units):
        add_own(i)

    @pl.when(jnp.logical_not(own_far))
    def _():
        last_relays()

    @pl.when(jnp.logical_not(jnp.logical_or(late_soon, late_last)))
    def _():
        form_late()

    def wait_heads(d, i):
        for j in range(i * unit_heads, (i + 1) * unit_heads):
            if j == heads - 1:
                for t in range(pieces):
                    tail_copy(n_seq - d, t).wait_recv()
            else:
                o_copy(n_seq - d, j).wait_recv()

    for i in range(own_units):
        for d in range(1, n_seq):
            if d == last_d and i == own_units - 1:
                continue
            wait_heads(d, i)
            owner = lax.rem(me_s + n_seq - d, n_seq)
            add_unit(
                att_buf[d * rows : (d + 1) * rows, i * unit : (i + 1) * unit], unit_rows(owner, i)
            )
    for r in range(0, rows, BLOCK):
        part = slice(r, r + BLOCK)
        base = proj_buf[part, :]
        base = base - jnp.mean(base, axis=-1, keepdims=True)
        base_sum[part, :] = jnp.broadcast_to(
            jnp.sum(base * base, axis=-1, keepdims=True), (BLOCK, LANES)
        )
        base_buf[part, :] = base.astype(jnp.bfloat16)
    sum_row[...] = base_sum[...].T[0:8, :]

    @pl.when(late_last)
    def _():
        form_late()

    base_prod[...] = lax.dot_general(
        rhs_buf[...], base_buf[...], nt, preferred_element_type=jnp.float32
    )

    own_width = channels // 2
    own_chan = pl.ds(pl.multiple_of(me_c * own_width, own_width), own_width)
    other_chan = pl.ds(pl.multiple_of(other * own_width, own_width), own_width)
    swap_rows = max(tail_rows, LANES)
    swaps = [
        remote(
            pred_buf.at[other_chan, s * swap_rows : (s + 1) * swap_rows],
            other_buf.at[:, s * swap_rows : (s + 1) * swap_rows],
            p_send, p_recv.at[s], cfg=other,
        )
        for s in range(rows // swap_rows)
    ]
    late_cols = slice((own_units - 1) * unit, own_units * unit)
    for j in range(heads - unit_heads, heads - 1):
        o_copy(n_seq - last_d, j).wait_recv()
    for t in range(pieces):
        tail_copy(n_seq - last_d, t).wait_recv()
        part = slice(t * tail_rows, (t + 1) * tail_rows)
        first = last_d * rows + t * tail_rows
        late_out = att_buf[first : first + tail_rows, late_cols]
        added = lax.dot_general(tail_mat[...], late_out, nt, preferred_element_type=jnp.float32)
        cross = late_out.astype(jnp.float32).T * (added[split:, :] + 2.0 * base_prod[split:, part])
        square_sum = sum_row[0:1, part] + jnp.sum(cross, axis=0, keepdims=True)
        inverse = lax.rsqrt(jnp.maximum(square_sum, 0.0) * (1.0 / model) + norm_eps)
        linear = (added[0:channels, :] + base_prod[0:channels, part]) + (
            added[channels:split, :] + base_prod[channels:split, part]
        )
        pred_buf[:, part] = linear * inverse + const_col[:, 0:tail_rows]
        if (t + 1) * tail_rows % swap_rows == 0:
            swaps[(t + 1) * tail_rows // swap_rows - 1].start()

    live = me_s * rows + lax.broadcasted_iota(jnp.int32, (own_width, rows), 1) < length

    drain(qkv_buf.at[:, rows:total, :], in_send)
    drain(o_buf, o_send)
    at_end = jnp.logical_or(place == 0, place == line_len - 1)

    @pl.when(at_end)
    def _():
        drain(w_buf.at[0 : 3 * line_len * half, :], w_send)

    @pl.when(jnp.logical_not(at_end))
    def _():
        drain(w_buf, w_send)

    is_cond = me_c == 0
    for s, swap in enumerate(swaps):
        part = slice(s * swap_rows, (s + 1) * swap_rows)
        swap.wait_recv()
        own_cols, other_cols = pred_buf[own_chan, part], other_buf[:, part]
        cond = jnp.where(is_cond, own_cols, other_cols)
        uncond = jnp.where(is_cond, other_cols, own_cols)
        base_ref[:, part] = jnp.where(live[:, part], uncond, 0.0)
        gain_ref[:, part] = jnp.where(live[:, part], cond - uncond, 0.0)
    drain(pred_buf.at[own_chan, :], p_send)


def solution(mesh):
    n_seq, n_req = mesh.shape["seq"], mesh.shape["req"]

    def on_device(
        queries,
        key_vectors,
        values,
        hidden,
        out_proj,
        head_weight,
        head_bias,
        attn_gate,
        shift_scale,
        grid_shape,
        step_index,
        guide_scale,
        latent,
    ):
        rows, width = queries.shape[2:]
        model = hidden.shape[3]
        channels = head_weight.shape[1]
        own_width = latent.shape[2]
        group = width // n_seq
        heads = group // HEAD_DIM
        line_len = n_req // 2
        total = n_seq * rows
        half = out_proj.shape[0] // 2
        subs = half // 16
        tail_rows = 128
        pieces = rows // tail_rows
        swaps = rows // max(tail_rows, LANES)
        unit = max(HEAD_DIM, 2 * out_proj.shape[0])
        hbm = pl.BlockSpec(memory_space=pltpu.HBM)
        dma = pltpu.SemaphoreType.DMA
        base, gain = pl.pallas_call(
            functools.partial(kernel, n_seq, n_req, tail_rows),
            out_shape=(pltpu.VMEM((own_width, rows), jnp.float32), pltpu.VMEM((own_width, rows), jnp.float32)),
            in_specs=[hbm] * 10,
            out_specs=(pl.BlockSpec(memory_space=pltpu.VMEM), pl.BlockSpec(memory_space=pltpu.VMEM)),
            scratch_shapes=[
                pltpu.VMEM((3, total, group), jnp.bfloat16),
                pltpu.VMEM((total, HEAD_DIM), jnp.bfloat16),
                pltpu.VMEM((total - rows, group), jnp.bfloat16),
                pltpu.VMEM((total, group), jnp.bfloat16),
                pltpu.VMEM((rows, model), jnp.bfloat16),
                pltpu.VMEM((width, model), jnp.bfloat16),
                pltpu.VMEM((total, HEAD_DIM), jnp.float32),
                pltpu.VMEM((total, HEAD_DIM), jnp.float32),
                pltpu.VMEM((channels, rows), jnp.float32),
                pltpu.VMEM((own_width, rows), jnp.float32),
                pltpu.VMEM((rows, model), jnp.float32),
                pltpu.VMEM((channels, model), jnp.bfloat16),
                pltpu.VMEM((1, channels), jnp.float32),
                pltpu.VMEM((channels, LANES), jnp.float32),
                pltpu.VMEM((2 * channels + unit, model), jnp.bfloat16),
                pltpu.VMEM((2 * channels + unit, unit), jnp.bfloat16),
                pltpu.VMEM((2 * channels + unit, rows), jnp.float32),
                pltpu.VMEM((rows, LANES), jnp.float32),
                pltpu.VMEM((8, rows), jnp.float32),
                pltpu.VMEM((rows, model), jnp.bfloat16),
                pltpu.VMEM((1, model), jnp.float32),
                pltpu.VMEM((2, model), jnp.float32),
                pltpu.SMEM((1, 3), jnp.int32),
                dma((8,)),
                pltpu.SemaphoreType.REGULAR((3,)),
                dma(()),
                dma((n_seq - 1, heads)),
                dma(()),
                dma((n_seq - 1, heads - 1 + pieces)),
                dma(()),
                dma((line_len, subs)),
                dma((line_len, subs)),
                dma((line_len,)),
                dma(()),
                dma((swaps,)),
            ],
            compiler_params=pltpu.CompilerParams(
                collective_id=0, has_side_effects=True, vmem_limit_bytes=56 * 1024 * 1024
            ),
        )(
            queries[0, 0],
            key_vectors[0, 0],
            values[0, 0],
            hidden[0, 0],
            out_proj,
            head_weight.T,
            head_bias[None, :],
            attn_gate,
            shift_scale[0],
            grid_shape,
        )
        step_value = step_index[0].astype(jnp.float32)
        delta = noise_level(step_value + 1.0) - noise_level(step_value)
        velocity = base + guide_scale[0] * gain
        next_latent = latent[0].T + delta * velocity
        return (next_latent.T[None], velocity.T[None])

    return jax.shard_map(
        on_device,
        mesh=mesh,
        in_specs=(
            P("req", "cfg", "seq", None),
            P("req", "cfg", "seq", None),
            P("req", "cfg", "seq", None),
            P("req", "cfg", "seq", None),
            P("req", None),
            P(),
            P(),
            P("req", None),
            P("req", None, None),
            P("req", None),
            P("req"),
            P("req"),
            P("req", "seq", "cfg"),
        ),
        out_specs=(P("req", "seq", "cfg"), P("req", "seq", "cfg")),
        check_vma=False,
    )
```
